32 devices in a mesh: leaf: 8 (over z, x), rhs: 4 (over y, core).
Axes of the slice: x: 2, y: 2, z: 4, core: 2. Of those that a mesh axis runs over, the one named last changes fastest.
Arguments:
- coords: bfloat16 [64, 32768], P(None, 'leaf'), may hold values from -1.5 to 1.5
- rhs: bfloat16 [256, 32768], P('rhs', 'leaf'), parts along dimension 0, may hold values from -6 to 6
- basis: bfloat16 [64, 512, 256], P('leaf'), may hold values from -0.25 to 0.25
- transfer_one: bfloat16 [32, 512, 256], P('leaf'), may hold values from -0.25 to 0.25
- transfer_two: bfloat16 [16, 512, 256], P('leaf'), may hold values from -0.25 to 0.25
- far_blocks: bfloat16 [112, 4, 256, 256], P('leaf'), may hold values from -0.375 to 0.375
- neighbours: int32 [64, 8], replicated, may hold values from 0 to 63, as said below
- far_lists: int32 [112, 4], replicated, may hold values from 0 to 111, as said below
Outputs:
- product: float32 [256, 32768], P('rhs', 'leaf'), parts along dimension 0
The draws below stay inside these ranges and needn't reach their ends.
There are 4 independent parts, one for each index of `rhs`. The reference program is written for one: setup_inputs(seed, part) draws one part's arguments, and reference() takes and returns one part's arrays. A program takes and returns all parts, laid end to end along the dimension named above; an argument that names none is the same for every part. Nothing has to cross between parts.
Inputs may be any that keep to these rules, and one draw needn't show every extreme that they name: `neighbours`: row i starts with leaf i itself; its other entries name leaves of other devices (leaf i lies on device i // 8). The entries after the first in the lists of one device's leaves name no other device more than 8 times, and the leaves of every device are named exactly 56 times by such entries over all lists. `far_lists`: entry (n, f) names a node of the same level as node n on another device (node n lies on device n // 14). The entries of one device's nodes name no other device more than 8 times, and the nodes of every device are named exactly 56 times over all entries.
All inputs are finite; a program needn't handle non-finite values.
Results may differ from the reference program's by a relative error of at most 0.005.
Values may be sent and summed in bfloat16 or wider, within the bound.
A program may use at most 128 MiB of HBM per device.

```python
import jax
import jax.numpy as jnp
from jax import lax

FEAT = 64
RANK = 256
R = 64
LEAF = 512
NB = 8
FAR = 4
LEAF_DEV = 8
LEAVES = 64
POINTS = 32768
NODE_DEV = 14
NODES = 112
N_LEAF = 8


def peer_targets(key, entry_count, peer_count):
    first_key, second_key = jax.random.split(key)
    placing = jax.random.permutation(first_key, peer_count).astype(jnp.int32)
    inverse = jnp.argsort(placing).astype(jnp.int32)
    offsets = (jax.random.permutation(second_key, peer_count - 1) + 1).astype(jnp.int32)
    chosen = offsets[jnp.arange(entry_count, dtype=jnp.int32) % (peer_count - 1)]
    devices = jnp.arange(peer_count, dtype=jnp.int32)
    return placing[(inverse[devices][:, None] + chosen[None, :]) % peer_count]


def draw_neighbours(key, part):
    peer_count = LEAVES // LEAF_DEV
    entry_count = (NB - 1) * LEAF_DEV
    first_key, second_key = jax.random.split(jax.random.fold_in(key, 11))
    owners = peer_targets(first_key, entry_count, peer_count)
    picked = jax.random.randint(second_key, (peer_count, entry_count), 0, LEAF_DEV, dtype=jnp.int32)
    remote = (owners * LEAF_DEV + picked).reshape(LEAVES, NB - 1)
    itself = jnp.arange(LEAVES, dtype=jnp.int32)[:, None]
    return jnp.concatenate([itself, remote], axis=1).astype(jnp.int32)


def draw_far_lists(key, part):
    peer_count = LEAVES // LEAF_DEV
    entry_count = NODE_DEV * FAR
    first_key, second_key = jax.random.split(jax.random.fold_in(key, 23))
    owners = peer_targets(first_key, entry_count, peer_count)
    asking = jnp.arange(entry_count, dtype=jnp.int32) // FAR
    level_start = jnp.where(asking < LEAF_DEV, 0, jnp.where(asking < LEAF_DEV * 3 // 2, LEAF_DEV, LEAF_DEV * 3 // 2))
    level_width = jnp.where(asking < LEAF_DEV, LEAF_DEV, jnp.where(asking < LEAF_DEV * 3 // 2, LEAF_DEV // 2, LEAF_DEV // 4))
    raw_pick = jax.random.randint(second_key, (peer_count, entry_count), 0, 1 << 20, dtype=jnp.int32)
    remote = owners * NODE_DEV + level_start[None, :] + raw_pick % level_width[None, :]
    return remote.reshape(NODES, FAR).astype(jnp.int32)


def level_of(own_key, dims, cuts, least, largest):
    level, own = 1.0, jax.random.fold_in(own_key, 6)
    for position, shards_of in cuts:
        draws = jnp.exp(jax.random.uniform(jax.random.fold_in(own, position), (shards_of,), jnp.float32, least / len(cuts), largest / len(cuts)))
        level = level * jnp.repeat(draws, dims[position] // shards_of).reshape([-1 if axis == position else 1 for axis in range(len(dims))])
    return level


def noise(stream_key, dims, scale, limit, cuts=(), kind=jnp.bfloat16):
    values = scale * jax.random.normal(stream_key, dims, jnp.float32)
    if cuts:
        values = values * level_of(stream_key, dims, cuts, -0.22, 0.18)
    return jnp.clip(values, -limit, limit).astype(kind)


def setup_inputs(seed: int = 0, part: int = 0) -> dict:
    splits = jax.random.split(jax.random.key(seed), 9)
    own_keys = jax.random.split(jax.random.fold_in(splits[8], part), 9)
    return {
        "coords": noise(splits[0], (FEAT, POINTS), 0.25, 1.5, ((1, 8),)),
        "rhs": noise(own_keys[1], (R, POINTS), 1.0, 6.0, ((1, 8),)),
        "basis": noise(splits[2], (LEAVES, LEAF, RANK), LEAF ** -0.5, 0.25, ((0, 8),)),
        "transfer_one": noise(splits[3], (LEAVES // 2, 2 * RANK, RANK), (2 * RANK) ** -0.5, 0.25, ((0, 8),)),
        "transfer_two": noise(splits[4], (LEAVES // 4, 2 * RANK, RANK), (2 * RANK) ** -0.5, 0.25, ((0, 8),)),
        "far_blocks": noise(splits[5], (NODES, FAR, RANK, RANK), RANK ** -0.5, 0.375, ((0, 8),)),
        "neighbours": draw_neighbours(jax.random.fold_in(splits[8], 71), part),
        "far_lists": draw_far_lists(jax.random.fold_in(splits[8], 71), part),
    }


def round_half(values):
    return lax.optimization_barrier(values.astype(jnp.bfloat16))


def kernel_tiles(sources, targets):
    src_f = sources.astype(jnp.float32)
    dst_f = targets.astype(jnp.float32)
    inner = jnp.einsum("...fa,...fb->...ab", src_f, dst_f, precision=lax.Precision.HIGHEST)
    src_sq = jnp.sum(src_f * src_f, axis=-2)
    dst_sq = jnp.sum(dst_f * dst_f, axis=-2)
    return round_half(jnp.exp(inner - 0.5 * src_sq[..., :, None] - 0.5 * dst_sq[..., None, :]))


def join_pairs(skeleton):
    return skeleton.reshape(-1, 2, R, RANK).transpose(0, 2, 1, 3).reshape(-1, R, 2 * RANK)


def descend(parent, transfer, child_far):
    rounded = round_half(parent).astype(jnp.float32)
    spread = jnp.einsum("mrk,mjk->mrj", rounded, transfer.astype(jnp.float32), precision=lax.Precision.HIGHEST)
    spread = spread.reshape(-1, R, 2, RANK).transpose(0, 2, 1, 3).reshape(-1, R, RANK)
    return child_far + spread


def reference(coords, rhs, basis, transfer_one, transfer_two, far_blocks, neighbours, far_lists):
    points = coords.reshape(FEAT, LEAVES, LEAF).transpose(1, 0, 2)
    charges = rhs.reshape(R, LEAVES, LEAF).transpose(1, 0, 2)

    def near_leaf(index):
        listed = neighbours[index]
        kernel = kernel_tiles(points[listed], points[index][None])
        return jnp.einsum("nra,nab->rb", charges[listed].astype(jnp.float32), kernel.astype(jnp.float32), precision=lax.Precision.HIGHEST)

    near = lax.map(near_leaf, jnp.arange(LEAVES, dtype=jnp.int32))
    skel_zero = round_half(jnp.einsum("lra,lak->lrk", charges.astype(jnp.float32), basis.astype(jnp.float32), precision=lax.Precision.HIGHEST))
    skel_one = round_half(jnp.einsum("mrj,mjk->mrk", join_pairs(skel_zero).astype(jnp.float32), transfer_one.astype(jnp.float32), precision=lax.Precision.HIGHEST))
    skel_two = round_half(jnp.einsum("mrj,mjk->mrk", join_pairs(skel_one).astype(jnp.float32), transfer_two.astype(jnp.float32), precision=lax.Precision.HIGHEST))
    skeleton = jnp.concatenate([
        skel_zero.reshape(N_LEAF, LEAF_DEV, R, RANK),
        skel_one.reshape(N_LEAF, LEAF_DEV // 2, R, RANK),
        skel_two.reshape(N_LEAF, LEAF_DEV // 4, R, RANK)], axis=1).reshape(NODES, R, RANK)
    far = jnp.zeros((NODES, R, RANK), jnp.float32)
    for partner in range(FAR):
        weights = skeleton[far_lists[:, partner]].astype(jnp.float32)
        far = far + jnp.einsum("nrk,nkj->nrj", weights, far_blocks[:, partner].astype(jnp.float32), precision=lax.Precision.HIGHEST)
    far = far.reshape(N_LEAF, NODE_DEV, R, RANK)
    far_zero = far[:, :LEAF_DEV].reshape(LEAVES, R, RANK)
    far_one = far[:, LEAF_DEV:LEAF_DEV * 3 // 2].reshape(LEAVES // 2, R, RANK)
    far_two = far[:, LEAF_DEV * 3 // 2:].reshape(LEAVES // 4, R, RANK)
    middle = descend(far_two, transfer_two, far_one)
    lowest = descend(middle, transfer_one, far_zero)
    lowest_rounded = round_half(lowest).astype(jnp.float32)
    result = near + jnp.einsum("lrk,lak->lra", lowest_rounded, basis.astype(jnp.float32), precision=lax.Precision.HIGHEST)
    return result.transpose(1, 0, 2).reshape(R, POINTS)
```

```python
import functools

import jax
import jax.numpy as jnp
from jax import lax
from jax.experimental import pallas as pl
from jax.experimental.pallas import tpu as pltpu
from jax.sharding import PartitionSpec as P

FEAT = 64
RANK = 256
R = 64
LEAF = 512
NB = 8
FAR = 4


def kernel_tiles(sources, targets):
    inner = jnp.einsum("...fa,...fb->...ab", sources, targets, preferred_element_type=jnp.float32)
    src_f = sources.astype(jnp.float32)
    dst_f = targets.astype(jnp.float32)
    src_sq = jnp.sum(src_f * src_f, axis=-2)
    dst_sq = jnp.sum(dst_f * dst_f, axis=-2)
    return jnp.exp(inner - 0.5 * src_sq[..., :, None] - 0.5 * dst_sq[..., None, :]).astype(
        jnp.bfloat16
    )


def tile_products(sources, targets):
    kernel = kernel_tiles(sources[:, :FEAT], targets)
    return jnp.einsum("gra,gab->grb", sources[:, FEAT:], kernel, preferred_element_type=jnp.float32)


def grouped_products(sources, targets):
    groups = sources.shape[0] // 4
    paired = (
        sources.reshape(groups, 4, sources.shape[1], sources.shape[2]),
        targets.reshape(groups, 4, targets.shape[1], targets.shape[2]),
    )
    outcome = lax.map(lambda couple: tile_products(couple[0], couple[1]), paired)
    return outcome.reshape(sources.shape[0], R, sources.shape[2])


def slot_ranks(owners):
    entry_count = owners.shape[1]
    position = jnp.arange(entry_count, dtype=jnp.int32)
    earlier = position[None, :] < position[:, None]
    matches = owners[:, :, None] == owners[:, None, :]
    return jnp.sum(jnp.logical_and(matches, earlier[None]), axis=2)


def arrivals(owners, ranks, entries, device_index, slot_count):
    entry_count = owners.shape[1]
    located = jnp.nonzero((owners == device_index).reshape(-1), size=entry_count, fill_value=0)[
        0
    ].astype(jnp.int32)
    requester = located // entry_count
    target_slot = requester * slot_count + ranks.reshape(-1)[located]
    return (target_slot, entries.reshape(-1)[located])


def join_pairs(skeleton):
    return skeleton.reshape(-1, 2, R, RANK).transpose(0, 2, 1, 3).reshape(-1, R, 2 * RANK)


def descend(parent, transfer, child_far):
    rounded = parent.astype(jnp.bfloat16)
    spread = jnp.einsum("mrk,mjk->mrj", rounded, transfer, preferred_element_type=jnp.float32)
    spread = spread.reshape(-1, R, 2, RANK).transpose(0, 2, 1, 3).reshape(-1, R, RANK)
    return child_far + spread


def exchanged(coords, rhs, basis, transfer_one, transfer_two, far_blocks, neighbours, far_lists):
    peer_count = lax.axis_size("leaf")
    device_index = lax.axis_index("leaf")
    local_leaves = basis.shape[0]
    node_count = far_blocks.shape[0]
    remote_count = (NB - 1) * local_leaves
    near_slots = (remote_count + peer_count - 2) // (peer_count - 1)
    far_count = node_count * FAR
    far_slots = (far_count + peer_count - 2) // (peer_count - 1)
    points = coords.reshape(FEAT, local_leaves, LEAF).transpose(1, 0, 2)
    charges = rhs.reshape(R, local_leaves, LEAF).transpose(1, 0, 2)
    blocks = jnp.concatenate([points, charges], axis=1)
    remote = neighbours.reshape(peer_count, local_leaves, NB)[:, :, 1:].reshape(
        peer_count, remote_count
    )
    owners = remote // local_leaves
    ranks = slot_ranks(owners)
    my_owners = lax.dynamic_index_in_dim(owners, device_index, 0, keepdims=False)
    my_ranks = lax.dynamic_index_in_dim(ranks, device_index, 0, keepdims=False)
    my_slots = my_owners * near_slots + my_ranks
    outgoing, wanted = arrivals(owners, ranks, remote, device_index, near_slots)
    item_leaf = jnp.arange(remote_count, dtype=jnp.int32) // (NB - 1)
    skel_zero = jnp.einsum(
        "lra,lak->lrk", charges, basis, preferred_element_type=jnp.float32
    ).astype(jnp.bfloat16)
    skel_one = jnp.einsum(
        "mrj,mjk->mrk", join_pairs(skel_zero), transfer_one, preferred_element_type=jnp.float32
    ).astype(jnp.bfloat16)
    skel_two = jnp.einsum(
        "mrj,mjk->mrk", join_pairs(skel_one), transfer_two, preferred_element_type=jnp.float32
    ).astype(jnp.bfloat16)
    skeleton = jnp.concatenate([skel_zero, skel_one, skel_two], axis=0)
    far_remote = far_lists.reshape(peer_count, far_count)
    far_owners = far_remote // node_count
    far_ranks = slot_ranks(far_owners)
    far_outgoing, far_wanted = arrivals(far_owners, far_ranks, far_remote, device_index, far_slots)
    far_buffer = (
        jnp.zeros((peer_count * far_slots, R, RANK), jnp.bfloat16)
        .at[far_outgoing]
        .set(skeleton[far_wanted % node_count])
    )
    far_arrived = lax.all_to_all(
        far_buffer.reshape(peer_count, far_slots, R, RANK),
        "leaf",
        split_axis=0,
        concat_axis=0,
        tiled=True,
    )
    my_far = lax.dynamic_index_in_dim(
        far_owners, device_index, 0, keepdims=False
    ) * far_slots + lax.dynamic_index_in_dim(far_ranks, device_index, 0, keepdims=False)
    partners = far_arrived.reshape(peer_count * far_slots, R, RANK)[my_far].reshape(
        node_count, FAR, R, RANK
    )
    leaf_buffer = (
        jnp.zeros((peer_count * near_slots, FEAT + R, LEAF), jnp.bfloat16)
        .at[outgoing]
        .set(blocks[wanted % local_leaves])
    )
    leaf_arrived = lax.all_to_all(
        leaf_buffer.reshape(peer_count, near_slots, FEAT + R, LEAF),
        "leaf",
        split_axis=0,
        concat_axis=0,
        tiled=True,
    )
    sources = leaf_arrived.reshape(peer_count * near_slots, FEAT + R, LEAF)[my_slots]
    per_item = grouped_products(sources, points[item_leaf])
    self_terms = tile_products(blocks, points)
    near = self_terms + jnp.sum(per_item.reshape(local_leaves, NB - 1, R, LEAF), axis=1)
    far = jnp.einsum("nfrk,nfkj->nrj", partners, far_blocks, preferred_element_type=jnp.float32)
    far_zero = far[:local_leaves]
    far_one = far[local_leaves : local_leaves * 3 // 2]
    far_two = far[local_leaves * 3 // 2 :]
    middle = descend(far_two, transfer_two, far_one)
    lowest = descend(middle, transfer_one, far_zero)
    result = near + jnp.einsum(
        "lrk,lak->lra", lowest.astype(jnp.bfloat16), basis, preferred_element_type=jnp.float32
    )
    return result.transpose(1, 0, 2).reshape(R, local_leaves * LEAF)


def near_kernel(list_ref, *refs):
    sources, charges = refs[:NB], refs[NB : 2 * NB]
    target_ref, out_ref = refs[2 * NB], refs[2 * NB + 1]
    target = target_ref[...]
    target_f = target.astype(jnp.float32)
    target_half = 0.5 * jnp.sum(target_f * target_f, axis=0, keepdims=True)
    total = None
    for source_ref, charge_ref in zip(sources, charges):
        source = source_ref[...]
        source_f = source.astype(jnp.float32)
        source_half = 0.5 * jnp.sum(source_f * source_f, axis=0, keepdims=True)
        inner = lax.dot_general(
            source, target, (((0,), (0,)), ((), ())), preferred_element_type=jnp.float32
        )
        kernel = jnp.exp(inner - source_half.T - target_half).astype(jnp.bfloat16)
        term = jnp.dot(charge_ref[...], kernel, preferred_element_type=jnp.float32)
        total = term if total is None else total + term
    out_ref[...] = total


def near_products(listed, all_coords, all_rhs, coords):
    local_leaves = listed.shape[0]
    per_device = all_rhs.shape[2] // LEAF

    def picked(slot):
        def index(leaf, list_ref):
            chosen = list_ref[leaf, slot]
            return (chosen // per_device, 0, chosen % per_device)

        return index

    return pl.pallas_call(
        near_kernel,
        grid_spec=pltpu.PrefetchScalarGridSpec(
            num_scalar_prefetch=1,
            grid=(local_leaves,),
            in_specs=[pl.BlockSpec((None, FEAT, LEAF), picked(slot)) for slot in range(NB)]
            + [pl.BlockSpec((None, R, LEAF), picked(slot)) for slot in range(NB)]
            + [pl.BlockSpec((FEAT, LEAF), lambda leaf, list_ref: (0, leaf))],
            out_specs=pl.BlockSpec((R, LEAF), lambda leaf, list_ref: (0, leaf)),
        ),
        out_shape=jax.ShapeDtypeStruct((R, local_leaves * LEAF), jnp.float32),
        compiler_params=pltpu.CompilerParams(vmem_limit_bytes=32 * 1024 * 1024),
        cost_estimate=pl.CostEstimate(
            flops=local_leaves * NB * LEAF * LEAF * 1024,
            bytes_accessed=local_leaves * NB * LEAF * 256,
            transcendentals=local_leaves * NB * LEAF * LEAF,
        ),
        name="near",
    )(listed, *[all_coords] * NB, *[all_rhs] * NB, coords)


def far_kernel(list_ref, *refs):
    weights = refs[:FAR]
    block_ref, out_ref = refs[FAR], refs[FAR + 1]
    total = None
    for partner in range(FAR):
        term = jnp.dot(
            weights[partner][...], block_ref[partner], preferred_element_type=jnp.float32
        )
        total = term if total is None else total + term
    out_ref[...] = total


def far_products(listed, skeleton, far_blocks):
    node_count = listed.shape[0]

    def picked(partner):
        return lambda node, list_ref: (list_ref[node, partner], 0, 0)

    return pl.pallas_call(
        far_kernel,
        grid_spec=pltpu.PrefetchScalarGridSpec(
            num_scalar_prefetch=1,
            grid=(node_count,),
            in_specs=[pl.BlockSpec((None, R, RANK), picked(partner)) for partner in range(FAR)]
            + [pl.BlockSpec((None, FAR, RANK, RANK), lambda node, list_ref: (node, 0, 0, 0))],
            out_specs=pl.BlockSpec((None, R, RANK), lambda node, list_ref: (node, 0, 0)),
        ),
        out_shape=jax.ShapeDtypeStruct((node_count, R, RANK), jnp.float32),
        compiler_params=pltpu.CompilerParams(vmem_limit_bytes=32 * 1024 * 1024),
        cost_estimate=pl.CostEstimate(
            flops=node_count * FAR * 2 * R * RANK * RANK,
            bytes_accessed=node_count * FAR * (RANK + R) * RANK * 2,
            transcendentals=0,
        ),
        name="far",
    )(listed, *[skeleton] * FAR, far_blocks)


def on_device(coords, rhs, basis, transfer_one, transfer_two, far_blocks, neighbours, far_lists):
    peer_count = lax.axis_size("leaf")
    local_leaves = basis.shape[0]
    if (NB - 1) * local_leaves < (peer_count - 1) * local_leaves:
        return exchanged(
            coords, rhs, basis, transfer_one, transfer_two, far_blocks, neighbours, far_lists
        )
    return gathered(
        coords, rhs, basis, transfer_one, transfer_two, far_blocks, neighbours, far_lists
    )


def gathered(coords, rhs, basis, transfer_one, transfer_two, far_blocks, neighbours, far_lists):
    peer_count = lax.axis_size("leaf")
    parts = lax.axis_size("rhs")
    device_index = lax.axis_index("leaf")
    local_leaves = basis.shape[0]
    node_count = far_blocks.shape[0]
    columns = rhs.shape[1]
    all_rhs = lax.all_gather(rhs, "leaf")
    share = lax.dynamic_slice_in_dim(
        coords, lax.axis_index("rhs") * (FEAT // parts), FEAT // parts, 0
    )
    all_coords = lax.all_gather(share, ("leaf", "rhs")).reshape(peer_count, FEAT, columns)
    charges = rhs.reshape(R, local_leaves, LEAF).transpose(1, 0, 2)
    skel_zero = jnp.einsum(
        "lra,lak->lrk", charges, basis, preferred_element_type=jnp.float32
    ).astype(jnp.bfloat16)
    skel_one = jnp.einsum(
        "mrj,mjk->mrk", join_pairs(skel_zero), transfer_one, preferred_element_type=jnp.float32
    ).astype(jnp.bfloat16)
    skel_two = jnp.einsum(
        "mrj,mjk->mrk", join_pairs(skel_one), transfer_two, preferred_element_type=jnp.float32
    ).astype(jnp.bfloat16)
    skeleton = jnp.concatenate([skel_zero, skel_one, skel_two], axis=0)
    all_skeleton = lax.all_gather(skeleton, "leaf").reshape(peer_count * node_count, R, RANK)
    my_neighbours = lax.dynamic_slice_in_dim(neighbours, device_index * local_leaves, local_leaves, 0)
    my_far = lax.dynamic_slice_in_dim(far_lists, device_index * node_count, node_count, 0)
    near = near_products(my_neighbours, all_coords, all_rhs, coords)
    far = far_products(my_far, all_skeleton, far_blocks)
    far_zero = far[:local_leaves]
    far_one = far[local_leaves : local_leaves * 3 // 2]
    far_two = far[local_leaves * 3 // 2 :]
    middle = descend(far_two, transfer_two, far_one)
    lowest = descend(middle, transfer_one, far_zero)
    spread = jnp.einsum(
        "lrk,lak->lra", lowest.astype(jnp.bfloat16), basis, preferred_element_type=jnp.float32
    )
    return near + spread.transpose(1, 0, 2).reshape(R, local_leaves * LEAF)


def solution(mesh):
    return jax.shard_map(
        on_device,
        mesh=mesh,
        in_specs=(
            P(None, "leaf"),
            P("rhs", "leaf"),
            P("leaf", None, None),
            P("leaf", None, None),
            P("leaf", None, None),
            P("leaf", None, None, None),
            P(),
            P(),
        ),
        out_specs=P("rhs", "leaf"),
        check_vma=False,
    )
```

```python
import functools

import jax
import jax.numpy as jnp
from jax import lax
from jax.experimental import pallas as pl
from jax.experimental.pallas import tpu as pltpu
from jax.sharding import PartitionSpec as P

FEAT = 64
RANK = 256
R = 64
LEAF = 512
NB = 8
FAR = 4


def kernel_tiles(sources, targets):
    inner = jnp.einsum("...fa,...fb->...ab", sources, targets, preferred_element_type=jnp.float32)
    src_f = sources.astype(jnp.float32)
    dst_f = targets.astype(jnp.float32)
    src_sq = jnp.sum(src_f * src_f, axis=-2)
    dst_sq = jnp.sum(dst_f * dst_f, axis=-2)
    return jnp.exp(inner - 0.5 * src_sq[..., :, None] - 0.5 * dst_sq[..., None, :]).astype(
        jnp.bfloat16
    )


def tile_products(sources, targets):
    kernel = kernel_tiles(sources[:, :FEAT], targets)
    return jnp.einsum("gra,gab->grb", sources[:, FEAT:], kernel, preferred_element_type=jnp.float32)


def grouped_products(sources, targets):
    groups = sources.shape[0] // 4
    paired = (
        sources.reshape(groups, 4, sources.shape[1], sources.shape[2]),
        targets.reshape(groups, 4, targets.shape[1], targets.shape[2]),
    )
    outcome = lax.map(lambda couple: tile_products(couple[0], couple[1]), paired)
    return outcome.reshape(sources.shape[0], R, sources.shape[2])


def slot_ranks(owners):
    entry_count = owners.shape[1]
    position = jnp.arange(entry_count, dtype=jnp.int32)
    earlier = position[None, :] < position[:, None]
    matches = owners[:, :, None] == owners[:, None, :]
    return jnp.sum(jnp.logical_and(matches, earlier[None]), axis=2)


def arrivals(owners, ranks, entries, device_index, slot_count):
    entry_count = owners.shape[1]
    located = jnp.nonzero((owners == device_index).reshape(-1), size=entry_count, fill_value=0)[
        0
    ].astype(jnp.int32)
    requester = located // entry_count
    target_slot = requester * slot_count + ranks.reshape(-1)[located]
    return (target_slot, entries.reshape(-1)[located])


def join_pairs(skeleton):
    return skeleton.reshape(-1, 2, R, RANK).transpose(0, 2, 1, 3).reshape(-1, R, 2 * RANK)


def descend(parent, transfer, child_far):
    rounded = parent.astype(jnp.bfloat16)
    spread = jnp.einsum("mrk,mjk->mrj", rounded, transfer, preferred_element_type=jnp.float32)
    spread = spread.reshape(-1, R, 2, RANK).transpose(0, 2, 1, 3).reshape(-1, R, RANK)
    return child_far + spread


def exchanged(coords, rhs, basis, transfer_one, transfer_two, far_blocks, neighbours, far_lists):
    peer_count = lax.axis_size("leaf")
    device_index = lax.axis_index("leaf")
    local_leaves = basis.shape[0]
    node_count = far_blocks.shape[0]
    remote_count = (NB - 1) * local_leaves
    near_slots = (remote_count + peer_count - 2) // (peer_count - 1)
    far_count = node_count * FAR
    far_slots = (far_count + peer_count - 2) // (peer_count - 1)
    points = coords.reshape(FEAT, local_leaves, LEAF).transpose(1, 0, 2)
    charges = rhs.reshape(R, local_leaves, LEAF).transpose(1, 0, 2)
    blocks = jnp.concatenate([points, charges], axis=1)
    remote = neighbours.reshape(peer_count, local_leaves, NB)[:, :, 1:].reshape(
        peer_count, remote_count
    )
    owners = remote // local_leaves
    ranks = slot_ranks(owners)
    my_owners = lax.dynamic_index_in_dim(owners, device_index, 0, keepdims=False)
    my_ranks = lax.dynamic_index_in_dim(ranks, device_index, 0, keepdims=False)
    my_slots = my_owners * near_slots + my_ranks
    outgoing, wanted = arrivals(owners, ranks, remote, device_index, near_slots)
    item_leaf = jnp.arange(remote_count, dtype=jnp.int32) // (NB - 1)
    skel_zero = jnp.einsum(
        "lra,lak->lrk", charges, basis, preferred_element_type=jnp.float32
    ).astype(jnp.bfloat16)
    skel_one = jnp.einsum(
        "mrj,mjk->mrk", join_pairs(skel_zero), transfer_one, preferred_element_type=jnp.float32
    ).astype(jnp.bfloat16)
    skel_two = jnp.einsum(
        "mrj,mjk->mrk", join_pairs(skel_one), transfer_two, preferred_element_type=jnp.float32
    ).astype(jnp.bfloat16)
    skeleton = jnp.concatenate([skel_zero, skel_one, skel_two], axis=0)
    far_remote = far_lists.reshape(peer_count, far_count)
    far_owners = far_remote // node_count
    far_ranks = slot_ranks(far_owners)
    far_outgoing, far_wanted = arrivals(far_owners, far_ranks, far_remote, device_index, far_slots)
    far_buffer = (
        jnp.zeros((peer_count * far_slots, R, RANK), jnp.bfloat16)
        .at[far_outgoing]
        .set(skeleton[far_wanted % node_count])
    )
    far_arrived = lax.all_to_all(
        far_buffer.reshape(peer_count, far_slots, R, RANK),
        "leaf",
        split_axis=0,
        concat_axis=0,
        tiled=True,
    )
    my_far = lax.dynamic_index_in_dim(
        far_owners, device_index, 0, keepdims=False
    ) * far_slots + lax.dynamic_index_in_dim(far_ranks, device_index, 0, keepdims=False)
    partners = far_arrived.reshape(peer_count * far_slots, R, RANK)[my_far].reshape(
        node_count, FAR, R, RANK
    )
    leaf_buffer = (
        jnp.zeros((peer_count * near_slots, FEAT + R, LEAF), jnp.bfloat16)
        .at[outgoing]
        .set(blocks[wanted % local_leaves])
    )
    leaf_arrived = lax.all_to_all(
        leaf_buffer.reshape(peer_count, near_slots, FEAT + R, LEAF),
        "leaf",
        split_axis=0,
        concat_axis=0,
        tiled=True,
    )
    sources = leaf_arrived.reshape(peer_count * near_slots, FEAT + R, LEAF)[my_slots]
    per_item = grouped_products(sources, points[item_leaf])
    self_terms = tile_products(blocks, points)
    near = self_terms + jnp.sum(per_item.reshape(local_leaves, NB - 1, R, LEAF), axis=1)
    far = jnp.einsum("nfrk,nfkj->nrj", partners, far_blocks, preferred_element_type=jnp.float32)
    far_zero = far[:local_leaves]
    far_one = far[local_leaves : local_leaves * 3 // 2]
    far_two = far[local_leaves * 3 // 2 :]
    middle = descend(far_two, transfer_two, far_one)
    lowest = descend(middle, transfer_one, far_zero)
    result = near + jnp.einsum(
        "lrk,lak->lra", lowest.astype(jnp.bfloat16), basis, preferred_element_type=jnp.float32
    )
    return result.transpose(1, 0, 2).reshape(R, local_leaves * LEAF)


POINT, SKEL, CHARGE = 0, 1, 2


def visit_orders(rows):
    return [sorted(range(rows), key=lambda row: (abs(row - at), row)) for at in range(rows)]


def tile(source, target, target_half, charge):
    source_f = source.astype(jnp.float32)
    source_half = 0.5 * jnp.sum(source_f * source_f, axis=0, keepdims=True)
    inner = lax.dot_general(
        source, target, (((0,), (0,)), ((), ())), preferred_element_type=jnp.float32
    )
    kernel = jnp.exp(inner - source_half.T - target_half).astype(jnp.bfloat16)
    return jnp.dot(charge, kernel, preferred_element_type=jnp.float32)


def half_square(points):
    points_f = points.astype(jnp.float32)
    return 0.5 * jnp.sum(points_f * points_f, axis=0, keepdims=True)


def whole_kernel(
    rows, parts, source_tab, target_tab, place_tab, far_tab, coords, rhs, skeleton, basis_hbm,
    one_hbm, two_hbm, blocks_hbm, out, *scratch
):
    slots = 2 * rows
    points_at = (None,) + scratch[: slots - 1]
    charges_at = (None,) + scratch[slots - 1 : 2 * slots - 2]
    (
        skel_at, terms, far_at, basis, one, two, blocks, local_sem, send_sem, recv_sem,
        peer_send_sem, peer_recv_sem,
    ) = scratch[2 * slots - 2 :]
    orders = visit_orders(rows)
    local_leaves, node_count = basis.shape[0], blocks.shape[0]
    share = coords.shape[1] // parts
    leaf = lax.axis_index("leaf")
    row, side = leaf // 2, leaf % 2
    part = lax.axis_index("rhs")
    across = (row * 2 + 1 - side, part)

    loads = [
        pltpu.make_async_copy(source, target, local_sem.at[which])
        for which, (source, target) in enumerate(
            ((blocks_hbm, blocks), (basis_hbm, basis), (one_hbm, one), (two_hbm, two))
        )
    ]
    for load in loads:
        load.start()

    barrier = pltpu.get_barrier_semaphore()
    mesh_ids = pl.DeviceIdType.MESH
    partners = [across] + [(leaf, (part + away) % parts) for away in range(1, parts)]
    for partner in partners:
        pl.semaphore_signal(barrier, inc=1, device_id=partner, device_id_type=mesh_ids)

    @pl.when(row > 0)
    def _():
        pl.semaphore_signal(barrier, inc=1, device_id=(leaf - 2, part), device_id_type=mesh_ids)

    @pl.when(row < rows - 1)
    def _():
        pl.semaphore_signal(barrier, inc=1, device_id=(leaf + 2, part), device_id_type=mesh_ids)

    ahead = (row + rows - 1) // rows + (2 * rows - 2 - row) // rows
    pl.semaphore_wait(barrier, len(partners) + ahead)

    def mine(points):
        return points.at[:, pl.ds(pl.multiple_of(part * share, share), share), :]

    def held(kind, slot, own):
        if kind == POINT:
            if own and slot == 0:
                return mine(coords)
            return mine(points_at[slot])
        if kind == SKEL:
            if own and slot == 0:
                return skeleton
            return skel_at.at[pl.ds((slot - 1) * node_count, node_count)]
        return rhs if own and slot == 0 else charges_at[slot]

    def remote(kind, slot, way, to_slot, device):
        return pltpu.make_async_remote_copy(
            src_ref=held(kind, slot, True),
            dst_ref=held(kind, to_slot, False),
            send_sem=send_sem.at[kind, slot, way],
            recv_sem=recv_sem.at[kind, to_slot],
            device_id=device,
            device_id_type=mesh_ids,
        )

    def to_peer(slot, away):
        return pltpu.make_async_remote_copy(
            src_ref=mine(points_at[slot]),
            dst_ref=mine(points_at[slot]),
            send_sem=peer_send_sem.at[slot, away - 1],
            recv_sem=peer_recv_sem.at[slot, away - 1],
            device_id=(leaf, (part + away) % parts),
            device_id_type=mesh_ids,
        )

    def sends(at, kind, slot):
        beside, rank = divmod(slot, rows)
        origin = orders[at][rank]
        found = []
        if kind == POINT or beside == 0:
            if origin <= at < rows - 1:
                to_slot = beside * rows + orders[at + 1].index(origin)
                found.append(remote(kind, slot, 0, to_slot, (leaf + 2, part)))
            if origin >= at > 0:
                to_slot = beside * rows + orders[at - 1].index(origin)
                found.append(remote(kind, slot, 1, to_slot, (leaf - 2, part)))
        if (beside == 0 and kind != POINT) or slot == 0:
            found.append(remote(kind, slot, 2, rows + rank, across))
        if kind == POINT and slot > 0:
            found.extend(to_peer(slot, away) for away in range(1, parts))
        return found

    def arrived(kind, slot):
        remote(kind, slot, 2, slot, across).wait_recv()

    def pass_on(at, kind, slot):
        arrived(kind, slot)
        for copy in sends(at, kind, slot):
            copy.start()

    def phase(at, distance):
        if distance == 0:
            for kind in (POINT, SKEL, CHARGE):
                for copy in sends(at, kind, 0):
                    copy.start()
            return
        if distance == 1:
            pass_on(at, POINT, rows)
        ranks = [rank for rank in range(rows) if abs(orders[at][rank] - at) == distance]
        for kind in (POINT, SKEL, CHARGE):
            for rank in ranks:
                pass_on(at, kind, rank)
        for rank in ranks:
            pass_on(at, POINT, rows + rank)

    def by_row(action):
        for at in range(rows):
            pl.when(row == at)(functools.partial(action, at))

    def tiles(slot):
        for away in range(1, parts):
            to_peer(slot, away).wait_recv()
        if slot >= rows:
            arrived(CHARGE, slot)
        first = (slot - 1) * local_leaves

        def entry(index, carry):
            where = first + index
            source = points_at[slot][source_tab[where]]
            target = coords[target_tab[where]]
            charge = charges_at[slot][source_tab[where]]
            terms[where] = tile(source, target, half_square(target), charge)
            return carry

        lax.fori_loop(0, local_leaves, entry, 0, unroll=UNROLL)

    by_row(functools.partial(phase, distance=0))

    own_first = (slots - 1) * local_leaves

    def own_entry(index, carry):
        target = coords[index]
        terms[own_first + index] = tile(target, target, half_square(target), rhs[index])
        return carry

    lax.fori_loop(0, local_leaves, own_entry, 0, unroll=UNROLL)
    for distance in range(1, rows):
        by_row(functools.partial(phase, distance=distance))
        tiles(distance)
        tiles(rows + distance - 1)

    for load in loads:
        load.wait()
    for slot in range(rows, slots):
        arrived(SKEL, slot)

    def far_node(node, carry):
        total = None
        for partner in range(FAR):
            weights = skel_at[far_tab[node * FAR + partner]]
            term = jnp.dot(weights, blocks[node, partner], preferred_element_type=jnp.float32)
            total = term if total is None else total + term
        far_at[node] = total
        return carry

    lax.fori_loop(0, node_count, far_node, 0, unroll=2)

    def spread_to(parent, transfer):
        return lax.dot_general(
            parent.astype(jnp.bfloat16), transfer, (((1,), (1,)), ((), ())),
            preferred_element_type=jnp.float32,
        )

    first_one, first_two = local_leaves, local_leaves * 3 // 2
    for parent in range(node_count - first_two):
        spread = spread_to(far_at[first_two + parent], two[parent])
        for child in range(2):
            far_at[first_one + 2 * parent + child] += spread[:, child * RANK : (child + 1) * RANK]
    for parent in range(first_two - first_one):
        spread = spread_to(far_at[first_one + parent], one[parent])
        for child in range(2):
            far_at[2 * parent + child] += spread[:, child * RANK : (child + 1) * RANK]

    tiles(slots - 1)

    for index in range(local_leaves):
        total = terms[own_first + index]
        for listed in range(NB - 1):
            total = total + terms[place_tab[index * (NB - 1) + listed]]
        out[:, index * LEAF : (index + 1) * LEAF] = total + spread_to(far_at[index], basis[index])

    def finish(at):
        for kind in (POINT, SKEL, CHARGE):
            for slot in range(slots):
                for copy in sends(at, kind, slot):
                    copy.wait_send()

    by_row(finish)


UNROLL = 2


def on_device(coords, rhs, basis, transfer_one, transfer_two, far_blocks, neighbours, far_lists):
    peer_count = lax.axis_size("leaf")
    whole_lists = peer_count == NB and peer_count % 2 == 0
    route = gathered if whole_lists and FEAT % lax.axis_size("rhs") == 0 else exchanged
    return route(coords, rhs, basis, transfer_one, transfer_two, far_blocks, neighbours, far_lists)


def gathered(coords, rhs, basis, transfer_one, transfer_two, far_blocks, neighbours, far_lists):
    peer_count = lax.axis_size("leaf")
    parts = lax.axis_size("rhs")
    rows = peer_count // 2
    device_index = lax.axis_index("leaf")
    local_leaves = basis.shape[0]
    node_count = far_blocks.shape[0]
    width = rhs.shape[1]
    remote_count = (NB - 1) * local_leaves
    points = coords.reshape(FEAT, local_leaves, LEAF).transpose(1, 0, 2)
    charges = rhs.reshape(R, local_leaves, LEAF).transpose(1, 0, 2)
    skel_zero = jnp.einsum(
        "lra,lak->lrk", charges, basis, preferred_element_type=jnp.float32
    ).astype(jnp.bfloat16)
    skel_one = jnp.einsum(
        "mrj,mjk->mrk", join_pairs(skel_zero), transfer_one, preferred_element_type=jnp.float32
    ).astype(jnp.bfloat16)
    skel_two = jnp.einsum(
        "mrj,mjk->mrk", join_pairs(skel_one), transfer_two, preferred_element_type=jnp.float32
    ).astype(jnp.bfloat16)
    skeleton = jnp.concatenate([skel_zero, skel_one, skel_two], axis=0)

    orders = visit_orders(rows)
    row, side = device_index // 2, device_index % 2

    def slot_of(owner):
        origin, beside = owner // 2, (owner % 2 + side) % 2
        rank = jnp.zeros_like(owner)
        for at in range(rows):
            for place in range(rows):
                matches = jnp.logical_and(row == at, origin == orders[at][place])
                rank = jnp.where(matches, place, rank)
        return beside * rows + rank

    listed = lax.dynamic_slice_in_dim(neighbours, device_index * local_leaves, local_leaves, 0)
    remote = listed[:, 1:].reshape(remote_count)
    slot = slot_of(remote // local_leaves)
    position = jnp.arange(remote_count, dtype=jnp.int32)
    earlier = jnp.logical_and(slot[:, None] == slot[None, :], position[None, :] < position[:, None])
    place_tab = (slot - 1) * local_leaves + jnp.sum(earlier, axis=1, dtype=jnp.int32)
    chosen = place_tab[None, :] == position[:, None]
    source_tab = jnp.sum(jnp.where(chosen, (remote % local_leaves)[None, :], 0), axis=1)
    target_tab = jnp.sum(jnp.where(chosen, (position // (NB - 1))[None, :], 0), axis=1)
    far_listed = lax.dynamic_slice_in_dim(far_lists, device_index * node_count, node_count, 0)
    far_listed = far_listed.reshape(node_count * FAR)
    far_tab = (slot_of(far_listed // node_count) - 1) * node_count + far_listed % node_count

    smem = pl.BlockSpec(memory_space=pltpu.SMEM)
    vmem = pl.BlockSpec(memory_space=pltpu.VMEM)
    anywhere = pl.BlockSpec(memory_space=pl.ANY)
    remote_slots = peer_count - 1
    bf16 = jnp.bfloat16
    return pl.pallas_call(
        functools.partial(whole_kernel, rows, parts),
        out_shape=jax.ShapeDtypeStruct((R, width), jnp.float32),
        in_specs=[smem] * 4 + [vmem] * 3 + [anywhere] * 4,
        out_specs=vmem,
        scratch_shapes=[pltpu.VMEM((local_leaves, FEAT, LEAF), bf16)] * remote_slots
        + [pltpu.VMEM((local_leaves, R, LEAF), bf16)] * remote_slots
        + [
            pltpu.VMEM((remote_slots * node_count, R, RANK), bf16),
            pltpu.VMEM((peer_count * local_leaves, R, LEAF), jnp.float32),
            pltpu.VMEM((node_count, R, RANK), jnp.float32),
            pltpu.VMEM(basis.shape, bf16),
            pltpu.VMEM(transfer_one.shape, bf16),
            pltpu.VMEM(transfer_two.shape, bf16),
            pltpu.VMEM(far_blocks.shape, bf16),
            pltpu.SemaphoreType.DMA((4,)),
            pltpu.SemaphoreType.DMA((3, peer_count, 3)),
            pltpu.SemaphoreType.DMA((3, peer_count)),
            pltpu.SemaphoreType.DMA((peer_count, parts - 1)),
            pltpu.SemaphoreType.DMA((peer_count, parts - 1)),
        ],
        compiler_params=pltpu.CompilerParams(
            collective_id=0, has_side_effects=True, vmem_limit_bytes=56 * 1024 * 1024
        ),
        name="whole",
    )(
        source_tab, target_tab, place_tab, far_tab, points, charges, skeleton, basis, transfer_one,
        transfer_two, far_blocks,
    )


def solution(mesh):
    return jax.shard_map(
        on_device,
        mesh=mesh,
        in_specs=(
            P(None, "leaf"),
            P("rhs", "leaf"),
            P("leaf", None, None),
            P("leaf", None, None),
            P("leaf", None, None),
            P("leaf", None, None, None),
            P(),
            P(),
        ),
        out_specs=P("rhs", "leaf"),
        check_vma=False,
    )
```

```python
import functools

import jax
import jax.numpy as jnp
from jax import lax
from jax.experimental import pallas as pl
from jax.experimental.pallas import tpu as pltpu
from jax.sharding import PartitionSpec as P

FEAT = 64
RANK = 256
R = 64
LEAF = 512
NB = 8
FAR = 4


def kernel_tiles(sources, targets):
    inner = jnp.einsum("...fa,...fb->...ab", sources, targets, preferred_element_type=jnp.float32)
    src_f = sources.astype(jnp.float32)
    dst_f = targets.astype(jnp.float32)
    src_sq = jnp.sum(src_f * src_f, axis=-2)
    dst_sq = jnp.sum(dst_f * dst_f, axis=-2)
    return jnp.exp(inner - 0.5 * src_sq[..., :, None] - 0.5 * dst_sq[..., None, :]).astype(
        jnp.bfloat16
    )


def tile_products(sources, targets):
    kernel = kernel_tiles(sources[:, :FEAT], targets)
    return jnp.einsum("gra,gab->grb", sources[:, FEAT:], kernel, preferred_element_type=jnp.float32)


def grouped_products(sources, targets):
    groups = sources.shape[0] // 4
    paired = (
        sources.reshape(groups, 4, sources.shape[1], sources.shape[2]),
        targets.reshape(groups, 4, targets.shape[1], targets.shape[2]),
    )
    outcome = lax.map(lambda couple: tile_products(couple[0], couple[1]), paired)
    return outcome.reshape(sources.shape[0], R, sources.shape[2])


def slot_ranks(owners):
    entry_count = owners.shape[1]
    position = jnp.arange(entry_count, dtype=jnp.int32)
    earlier = position[None, :] < position[:, None]
    matches = owners[:, :, None] == owners[:, None, :]
    return jnp.sum(jnp.logical_and(matches, earlier[None]), axis=2)


def arrivals(owners, ranks, entries, device_index, slot_count):
    entry_count = owners.shape[1]
    located = jnp.nonzero((owners == device_index).reshape(-1), size=entry_count, fill_value=0)[
        0
    ].astype(jnp.int32)
    requester = located // entry_count
    target_slot = requester * slot_count + ranks.reshape(-1)[located]
    return (target_slot, entries.reshape(-1)[located])


def join_pairs(skeleton):
    return skeleton.reshape(-1, 2, R, RANK).transpose(0, 2, 1, 3).reshape(-1, R, 2 * RANK)


def descend(parent, transfer, child_far):
    rounded = parent.astype(jnp.bfloat16)
    spread = jnp.einsum("mrk,mjk->mrj", rounded, transfer, preferred_element_type=jnp.float32)
    spread = spread.reshape(-1, R, 2, RANK).transpose(0, 2, 1, 3).reshape(-1, R, RANK)
    return child_far + spread


def exchanged(coords, rhs, basis, transfer_one, transfer_two, far_blocks, neighbours, far_lists):
    peer_count = lax.axis_size("leaf")
    device_index = lax.axis_index("leaf")
    local_leaves = basis.shape[0]
    node_count = far_blocks.shape[0]
    remote_count = (NB - 1) * local_leaves
    near_slots = (remote_count + peer_count - 2) // (peer_count - 1)
    far_count = node_count * FAR
    far_slots = (far_count + peer_count - 2) // (peer_count - 1)
    points = coords.reshape(FEAT, local_leaves, LEAF).transpose(1, 0, 2)
    charges = rhs.reshape(R, local_leaves, LEAF).transpose(1, 0, 2)
    blocks = jnp.concatenate([points, charges], axis=1)
    remote = neighbours.reshape(peer_count, local_leaves, NB)[:, :, 1:].reshape(
        peer_count, remote_count
    )
    owners = remote // local_leaves
    ranks = slot_ranks(owners)
    my_owners = lax.dynamic_index_in_dim(owners, device_index, 0, keepdims=False)
    my_ranks = lax.dynamic_index_in_dim(ranks, device_index, 0, keepdims=False)
    my_slots = my_owners * near_slots + my_ranks
    outgoing, wanted = arrivals(owners, ranks, remote, device_index, near_slots)
    item_leaf = jnp.arange(remote_count, dtype=jnp.int32) // (NB - 1)
    skel_zero = jnp.einsum(
        "lra,lak->lrk", charges, basis, preferred_element_type=jnp.float32
    ).astype(jnp.bfloat16)
    skel_one = jnp.einsum(
        "mrj,mjk->mrk", join_pairs(skel_zero), transfer_one, preferred_element_type=jnp.float32
    ).astype(jnp.bfloat16)
    skel_two = jnp.einsum(
        "mrj,mjk->mrk", join_pairs(skel_one), transfer_two, preferred_element_type=jnp.float32
    ).astype(jnp.bfloat16)
    skeleton = jnp.concatenate([skel_zero, skel_one, skel_two], axis=0)
    far_remote = far_lists.reshape(peer_count, far_count)
    far_owners = far_remote // node_count
    far_ranks = slot_ranks(far_owners)
    far_outgoing, far_wanted = arrivals(far_owners, far_ranks, far_remote, device_index, far_slots)
    far_buffer = (
        jnp.zeros((peer_count * far_slots, R, RANK), jnp.bfloat16)
        .at[far_outgoing]
        .set(skeleton[far_wanted % node_count])
    )
    far_arrived = lax.all_to_all(
        far_buffer.reshape(peer_count, far_slots, R, RANK),
        "leaf",
        split_axis=0,
        concat_axis=0,
        tiled=True,
    )
    my_far = lax.dynamic_index_in_dim(
        far_owners, device_index, 0, keepdims=False
    ) * far_slots + lax.dynamic_index_in_dim(far_ranks, device_index, 0, keepdims=False)
    partners = far_arrived.reshape(peer_count * far_slots, R, RANK)[my_far].reshape(
        node_count, FAR, R, RANK
    )
    leaf_buffer = (
        jnp.zeros((peer_count * near_slots, FEAT + R, LEAF), jnp.bfloat16)
        .at[outgoing]
        .set(blocks[wanted % local_leaves])
    )
    leaf_arrived = lax.all_to_all(
        leaf_buffer.reshape(peer_count, near_slots, FEAT + R, LEAF),
        "leaf",
        split_axis=0,
        concat_axis=0,
        tiled=True,
    )
    sources = leaf_arrived.reshape(peer_count * near_slots, FEAT + R, LEAF)[my_slots]
    per_item = grouped_products(sources, points[item_leaf])
    self_terms = tile_products(blocks, points)
    near = self_terms + jnp.sum(per_item.reshape(local_leaves, NB - 1, R, LEAF), axis=1)
    far = jnp.einsum("nfrk,nfkj->nrj", partners, far_blocks, preferred_element_type=jnp.float32)
    far_zero = far[:local_leaves]
    far_one = far[local_leaves : local_leaves * 3 // 2]
    far_two = far[local_leaves * 3 // 2 :]
    middle = descend(far_two, transfer_two, far_one)
    lowest = descend(middle, transfer_one, far_zero)
    result = near + jnp.einsum(
        "lrk,lak->lra", lowest.astype(jnp.bfloat16), basis, preferred_element_type=jnp.float32
    )
    return result.transpose(1, 0, 2).reshape(R, local_leaves * LEAF)


POINT, EARLY, SKEL, LATE = 0, 1, 2, 3


def visit_orders(rows):
    return [sorted(range(rows), key=lambda row: (abs(row - at), row)) for at in range(rows)]


def tile(source, target, target_half, charge):
    source_f = source.astype(jnp.float32)
    source_half = 0.5 * jnp.sum(source_f * source_f, axis=0, keepdims=True)
    inner = lax.dot_general(
        source, target, (((0,), (0,)), ((), ())), preferred_element_type=jnp.float32
    )
    kernel = jnp.exp(inner - source_half.T - target_half).astype(jnp.bfloat16)
    return jnp.dot(charge, kernel, preferred_element_type=jnp.float32)


def half_square(points):
    points_f = points.astype(jnp.float32)
    return 0.5 * jnp.sum(points_f * points_f, axis=0, keepdims=True)


def whole_kernel(
    rows, parts, source_tab, target_tab, place_tab, pick_tab, give_tab, far_tab, coords, rhs, basis_hbm,
    one_hbm, two_hbm, blocks_hbm, out, *scratch
):
    slots = 2 * rows
    points_at = (None,) + scratch[: slots - 1]
    charges_at = (None,) + scratch[slots - 1 : 2 * slots - 2]
    skel_at = scratch[2 * slots - 2 : 2 * slots - 2 + rows]
    (
        given, partners_at, terms, far_at, basis, one, two, blocks, local_sem, send_sem,
        recv_sem, peer_send_sem, peer_recv_sem,
    ) = scratch[2 * slots - 2 + rows :]
    orders = visit_orders(rows)
    local_leaves, node_count = basis.shape[0], blocks.shape[0]
    share = coords.shape[1] // parts
    leaf = lax.axis_index("leaf")
    row, side = leaf // 2, leaf % 2
    part = lax.axis_index("rhs")
    across = (row * 2 + 1 - side, part)

    loads = [
        pltpu.make_async_copy(source, target, local_sem.at[which])
        for which, (source, target) in enumerate(
            ((basis_hbm, basis), (one_hbm, one), (two_hbm, two), (blocks_hbm, blocks))
        )
    ]
    for load in loads:
        load.start()

    barrier = pltpu.get_barrier_semaphore()
    mesh_ids = pl.DeviceIdType.MESH
    partners = [across] + [(leaf, (part + away) % parts) for away in range(1, parts)]
    for partner in partners:
        pl.semaphore_signal(barrier, inc=1, device_id=partner, device_id_type=mesh_ids)

    @pl.when(row > 0)
    def _():
        pl.semaphore_signal(barrier, inc=1, device_id=(leaf - 2, part), device_id_type=mesh_ids)

    @pl.when(row < rows - 1)
    def _():
        pl.semaphore_signal(barrier, inc=1, device_id=(leaf + 2, part), device_id_type=mesh_ids)

    ahead = (row + rows - 1) // rows + (2 * rows - 2 - row) // rows
    pl.semaphore_wait(barrier, len(partners) + ahead)

    def mine(points):
        return points.at[:, pl.ds(pl.multiple_of(part * share, share), share), :]

    def far_part(rank):
        return pl.ds(rank * local_leaves, local_leaves)

    def held(kind, slot, own, over):
        if kind == POINT:
            return mine(coords if own and slot == 0 else points_at[slot])
        if kind == SKEL:
            if over:
                return given.at[far_part(slot)] if own else partners_at.at[far_part(slot - 1)]
            return skel_at[slot]
        half = local_leaves // 2
        part_at = pl.ds(0, half) if kind == EARLY else pl.ds(half, local_leaves - half)
        return (rhs if own and slot == 0 else charges_at[slot]).at[part_at]

    def remote(kind, slot, way, to_slot, device):
        return pltpu.make_async_remote_copy(
            src_ref=held(kind, slot, True, way == 2),
            dst_ref=held(kind, to_slot, False, way == 2),
            send_sem=send_sem.at[kind, slot, way],
            recv_sem=recv_sem.at[kind, to_slot],
            device_id=device,
            device_id_type=mesh_ids,
        )

    def to_peer(slot, away):
        return pltpu.make_async_remote_copy(
            src_ref=mine(points_at[slot]),
            dst_ref=mine(points_at[slot]),
            send_sem=peer_send_sem.at[slot, away - 1],
            recv_sem=peer_recv_sem.at[slot, away - 1],
            device_id=(leaf, (part + away) % parts),
            device_id_type=mesh_ids,
        )

    def along(at, kind, slot):
        origin = orders[at][slot]
        found = []
        if origin <= at < rows - 1:
            to_slot = orders[at + 1].index(origin)
            found.append(remote(kind, slot, 0, to_slot, (leaf + 2, part)))
        if origin >= at > 0:
            to_slot = orders[at - 1].index(origin)
            found.append(remote(kind, slot, 1, to_slot, (leaf - 2, part)))
        return found

    def beside(kind, slot):
        return remote(kind, slot, 2, rows + slot, across)

    def arrived(kind, slot):
        if slot < rows:
            remote(kind, 0, 0, slot, across).wait_recv()
        else:
            remote(kind, slot - rows, 2, slot, across).wait_recv()

    def share_points(slot):
        for away in range(1, parts):
            to_peer(slot, away).start()

    def choose(rank):
        def entry(index, carry):
            place = rank * local_leaves + index
            given[place] = skel_at[rank][give_tab[rows * local_leaves - local_leaves + place]]
            if rank > 0:
                taken = place - local_leaves
                partners_at[taken] = skel_at[rank][pick_tab[taken]]
            return carry

        lax.fori_loop(0, local_leaves, entry, 0)

    def start_along(kind, ranks, at):
        for rank in ranks:
            if at != orders[at][rank]:
                arrived(kind, rank)
            for copy in along(at, kind, rank):
                copy.start()

    def open_sends(at):
        for kind in (POINT, EARLY):
            start_along(kind, [0], at)
            beside(kind, 0).start()

    def more_sends(at):
        for kind in (SKEL, LATE):
            start_along(kind, [0], at)
            beside(kind, 0).start()

    def phase(at, distance):
        ranks = [rank for rank in range(rows) if abs(orders[at][rank] - at) == distance]
        for kind in (POINT, EARLY):
            start_along(kind, ranks, at)
            for rank in ranks:
                beside(kind, rank).start()
                if kind == POINT:
                    share_points(rank)
        start_along(SKEL, ranks, at)
        for rank in ranks:
            choose(rank)
        start_along(LATE, ranks, at)
        for rank in ranks:
            beside(SKEL, rank).start()
            beside(LATE, rank).start()

    def by_row(action):
        for at in range(rows):
            pl.when(row == at)(functools.partial(action, at))

    def tiles(slot):
        for away in range(1, parts):
            to_peer(slot, away).wait_recv()
        if slot >= rows:
            arrived(EARLY, slot)
            arrived(LATE, slot)
        first = (slot - 1) * local_leaves

        def entry(index, carry):
            where = first + index
            source = points_at[slot][source_tab[where]]
            target = coords[target_tab[where]]
            charge = charges_at[slot][source_tab[where]]
            terms[where] = tile(source, target, half_square(target), charge)
            return carry

        lax.fori_loop(0, local_leaves, entry, 0, unroll=UNROLL)

    by_row(open_sends)

    own_first = (slots - 1) * local_leaves

    def own_entry(index, carry):
        target = coords[index]
        terms[own_first + index] = tile(target, target, half_square(target), rhs[index])
        return carry

    for load in loads[:3]:
        load.wait()
    first_one, first_two = local_leaves, local_leaves * 3 // 2

    def joined(first, transfer):
        left = jnp.dot(
            skel_at[0][first], transfer[:RANK], preferred_element_type=jnp.float32
        )
        right = jnp.dot(
            skel_at[0][first + 1], transfer[RANK:], preferred_element_type=jnp.float32
        )
        return (left + right).astype(jnp.bfloat16)

    for index in range(local_leaves):
        skel_at[0][index] = jnp.dot(
            rhs[index], basis[index], preferred_element_type=jnp.float32
        ).astype(jnp.bfloat16)
    for index in range(first_two - first_one):
        skel_at[0][first_one + index] = joined(2 * index, one[index])
    for index in range(node_count - first_two):
        skel_at[0][first_two + index] = joined(first_one + 2 * index, two[index])
    choose(0)
    lax.fori_loop(0, local_leaves // 2, own_entry, 0, unroll=UNROLL)
    by_row(more_sends)
    lax.fori_loop(local_leaves // 2, local_leaves, own_entry, 0, unroll=UNROLL)
    for distance in range(1, rows):
        by_row(functools.partial(phase, distance=distance))
        arrived(POINT, rows + distance - 1)
        share_points(rows + distance - 1)
        tiles(distance)
        tiles(rows + distance - 1)

    loads[3].wait()
    arrived(POINT, slots - 1)
    share_points(slots - 1)
    for slot in range(rows, slots):
        arrived(SKEL, slot)

    def far_node(node, carry):
        total = None
        for partner in range(FAR):
            weights = partners_at[far_tab[node * FAR + partner]]
            term = jnp.dot(weights, blocks[node, partner], preferred_element_type=jnp.float32)
            total = term if total is None else total + term
        far_at[node] = total
        return carry

    lax.fori_loop(0, node_count, far_node, 0, unroll=2)

    def spread_to(parent, transfer):
        return lax.dot_general(
            parent.astype(jnp.bfloat16), transfer, (((1,), (1,)), ((), ())),
            preferred_element_type=jnp.float32,
        )

    for parent in range(node_count - first_two):
        spread = spread_to(far_at[first_two + parent], two[parent])
        for child in range(2):
            far_at[first_one + 2 * parent + child] += spread[:, child * RANK : (child + 1) * RANK]
    for parent in range(first_two - first_one):
        spread = spread_to(far_at[first_one + parent], one[parent])
        for child in range(2):
            far_at[2 * parent + child] += spread[:, child * RANK : (child + 1) * RANK]

    tiles(slots - 1)

    for index in range(local_leaves):
        total = terms[own_first + index]
        for listed in range(NB - 1):
            total = total + terms[place_tab[index * (NB - 1) + listed]]
        out[:, index * LEAF : (index + 1) * LEAF] = total + spread_to(far_at[index], basis[index])

    def finish(at):
        for kind in (POINT, EARLY, SKEL, LATE):
            for rank in range(rows):
                for copy in along(at, kind, rank):
                    copy.wait_send()

    by_row(finish)
    for rank in range(rows):
        for kind in (POINT, EARLY, SKEL, LATE):
            beside(kind, rank).wait_send()
    for slot in range(1, slots):
        for away in range(1, parts):
            to_peer(slot, away).wait_send()


UNROLL = 2


def on_device(coords, rhs, basis, transfer_one, transfer_two, far_blocks, neighbours, far_lists):
    peer_count = lax.axis_size("leaf")
    whole_lists = peer_count == NB and peer_count % 2 == 0
    even_lists = far_blocks.shape[0] * FAR == (NB - 1) * basis.shape[0]
    even_shares = FEAT % lax.axis_size("rhs") == 0
    route = gathered if whole_lists and even_lists and even_shares else exchanged
    return route(coords, rhs, basis, transfer_one, transfer_two, far_blocks, neighbours, far_lists)


def gathered(coords, rhs, basis, transfer_one, transfer_two, far_blocks, neighbours, far_lists):
    peer_count = lax.axis_size("leaf")
    parts = lax.axis_size("rhs")
    rows = peer_count // 2
    device_index = lax.axis_index("leaf")
    local_leaves = basis.shape[0]
    node_count = far_blocks.shape[0]
    width = rhs.shape[1]
    remote_count = (NB - 1) * local_leaves
    points = coords.reshape(FEAT, local_leaves, LEAF).transpose(1, 0, 2)
    charges = rhs.reshape(R, local_leaves, LEAF).transpose(1, 0, 2)
    orders = visit_orders(rows)
    row, side = device_index // 2, device_index % 2

    def slot_of(owner, side):
        origin, beside = owner // 2, (owner % 2 + side) % 2
        rank = jnp.zeros_like(owner)
        for at in range(rows):
            for place in range(rows):
                matches = jnp.logical_and(row == at, origin == orders[at][place])
                rank = jnp.where(matches, place, rank)
        return beside * rows + rank

    beside_index = device_index + 1 - 2 * side
    lists = jnp.stack(
        [
            neighbours.reshape(peer_count, local_leaves, NB)[:, :, 1:].reshape(peer_count, -1)[
                device_index
            ],
            far_lists.reshape(peer_count, node_count * FAR)[device_index],
            far_lists.reshape(peer_count, node_count * FAR)[beside_index],
        ]
    )
    widths = jnp.array([[local_leaves], [node_count], [node_count]], jnp.int32)
    sides = jnp.stack([side, side, 1 - side])[:, None]
    slot = slot_of(lists // widths, sides)
    position = jnp.arange(remote_count, dtype=jnp.int32)
    earlier = jnp.logical_and(
        slot[:, :, None] == slot[:, None, :], position[None, :] < position[:, None]
    )
    place = (slot - 1) * local_leaves + jnp.sum(earlier, axis=2, dtype=jnp.int32)
    chosen = place[:, None, :] == position[:, None]
    picks = jnp.sum(jnp.where(chosen, (lists % widths)[:, None, :], 0), axis=2)
    targets = jnp.sum(jnp.where(chosen[0], (position // (NB - 1))[None, :], 0), axis=1)
    tables = (picks[0], targets, place[0], picks[1], picks[2], place[1])

    smem = pl.BlockSpec(memory_space=pltpu.SMEM)
    vmem = pl.BlockSpec(memory_space=pltpu.VMEM)
    anywhere = pl.BlockSpec(memory_space=pl.ANY)
    remote_slots = peer_count - 1
    bf16 = jnp.bfloat16
    return pl.pallas_call(
        functools.partial(whole_kernel, rows, parts),
        out_shape=jax.ShapeDtypeStruct((R, width), jnp.float32),
        in_specs=[smem] * 6 + [vmem] * 2 + [anywhere] * 4,
        out_specs=vmem,
        scratch_shapes=[pltpu.VMEM((local_leaves, FEAT, LEAF), bf16)] * remote_slots
        + [pltpu.VMEM((local_leaves, R, LEAF), bf16)] * remote_slots
        + [pltpu.VMEM((node_count, R, RANK), bf16)] * rows
        + [
            pltpu.VMEM((rows * local_leaves, R, RANK), bf16),
            pltpu.VMEM((remote_count, R, RANK), bf16),
            pltpu.VMEM((peer_count * local_leaves, R, LEAF), jnp.float32),
            pltpu.VMEM((node_count, R, RANK), jnp.float32),
            pltpu.VMEM(basis.shape, bf16),
            pltpu.VMEM(transfer_one.shape, bf16),
            pltpu.VMEM(transfer_two.shape, bf16),
            pltpu.VMEM(far_blocks.shape, bf16),
            pltpu.SemaphoreType.DMA((4,)),
            pltpu.SemaphoreType.DMA((4, peer_count, 3)),
            pltpu.SemaphoreType.DMA((4, peer_count)),
            pltpu.SemaphoreType.DMA((peer_count, parts - 1)),
            pltpu.SemaphoreType.DMA((peer_count, parts - 1)),
        ],
        compiler_params=pltpu.CompilerParams(
            collective_id=0, has_side_effects=True, vmem_limit_bytes=56 * 1024 * 1024
        ),
        name="whole",
    )(
        *tables, points, charges, basis, transfer_one, transfer_two, far_blocks,
    )


def solution(mesh):
    return jax.shard_map(
        on_device,
        mesh=mesh,
        in_specs=(
            P(None, "leaf"),
            P("rhs", "leaf"),
            P("leaf", None, None),
            P("leaf", None, None),
            P("leaf", None, None),
            P("leaf", None, None, None),
            P(),
            P(),
        ),
        out_specs=P("rhs", "leaf"),
        check_vma=False,
    )
```

```python
import functools

import jax
import jax.numpy as jnp
from jax import lax
from jax.experimental import pallas as pl
from jax.experimental.pallas import tpu as pltpu
from jax.sharding import PartitionSpec as P

FEAT = 64
RANK = 256
R = 64
LEAF = 512
NB = 8
FAR = 4


def kernel_tiles(sources, targets):
    inner = jnp.einsum("...fa,...fb->...ab", sources, targets, preferred_element_type=jnp.float32)
    src_f = sources.astype(jnp.float32)
    dst_f = targets.astype(jnp.float32)
    src_sq = jnp.sum(src_f * src_f, axis=-2)
    dst_sq = jnp.sum(dst_f * dst_f, axis=-2)
    return jnp.exp(inner - 0.5 * src_sq[..., :, None] - 0.5 * dst_sq[..., None, :]).astype(
        jnp.bfloat16
    )


def tile_products(sources, targets):
    kernel = kernel_tiles(sources[:, :FEAT], targets)
    return jnp.einsum("gra,gab->grb", sources[:, FEAT:], kernel, preferred_element_type=jnp.float32)


def grouped_products(sources, targets):
    groups = sources.shape[0] // 4
    paired = (
        sources.reshape(groups, 4, sources.shape[1], sources.shape[2]),
        targets.reshape(groups, 4, targets.shape[1], targets.shape[2]),
    )
    outcome = lax.map(lambda couple: tile_products(couple[0], couple[1]), paired)
    return outcome.reshape(sources.shape[0], R, sources.shape[2])


def slot_ranks(owners):
    entry_count = owners.shape[1]
    position = jnp.arange(entry_count, dtype=jnp.int32)
    earlier = position[None, :] < position[:, None]
    matches = owners[:, :, None] == owners[:, None, :]
    return jnp.sum(jnp.logical_and(matches, earlier[None]), axis=2)


def arrivals(owners, ranks, entries, device_index, slot_count):
    entry_count = owners.shape[1]
    located = jnp.nonzero((owners == device_index).reshape(-1), size=entry_count, fill_value=0)[
        0
    ].astype(jnp.int32)
    requester = located // entry_count
    target_slot = requester * slot_count + ranks.reshape(-1)[located]
    return (target_slot, entries.reshape(-1)[located])


def join_pairs(skeleton):
    return skeleton.reshape(-1, 2, R, RANK).transpose(0, 2, 1, 3).reshape(-1, R, 2 * RANK)


def descend(parent, transfer, child_far):
    rounded = parent.astype(jnp.bfloat16)
    spread = jnp.einsum("mrk,mjk->mrj", rounded, transfer, preferred_element_type=jnp.float32)
    spread = spread.reshape(-1, R, 2, RANK).transpose(0, 2, 1, 3).reshape(-1, R, RANK)
    return child_far + spread


def exchanged(coords, rhs, basis, transfer_one, transfer_two, far_blocks, neighbours, far_lists):
    peer_count = lax.axis_size("leaf")
    device_index = lax.axis_index("leaf")
    local_leaves = basis.shape[0]
    node_count = far_blocks.shape[0]
    remote_count = (NB - 1) * local_leaves
    near_slots = (remote_count + peer_count - 2) // (peer_count - 1)
    far_count = node_count * FAR
    far_slots = (far_count + peer_count - 2) // (peer_count - 1)
    points = coords.reshape(FEAT, local_leaves, LEAF).transpose(1, 0, 2)
    charges = rhs.reshape(R, local_leaves, LEAF).transpose(1, 0, 2)
    blocks = jnp.concatenate([points, charges], axis=1)
    remote = neighbours.reshape(peer_count, local_leaves, NB)[:, :, 1:].reshape(
        peer_count, remote_count
    )
    owners = remote // local_leaves
    ranks = slot_ranks(owners)
    my_owners = lax.dynamic_index_in_dim(owners, device_index, 0, keepdims=False)
    my_ranks = lax.dynamic_index_in_dim(ranks, device_index, 0, keepdims=False)
    my_slots = my_owners * near_slots + my_ranks
    outgoing, wanted = arrivals(owners, ranks, remote, device_index, near_slots)
    item_leaf = jnp.arange(remote_count, dtype=jnp.int32) // (NB - 1)
    skel_zero = jnp.einsum(
        "lra,lak->lrk", charges, basis, preferred_element_type=jnp.float32
    ).astype(jnp.bfloat16)
    skel_one = jnp.einsum(
        "mrj,mjk->mrk", join_pairs(skel_zero), transfer_one, preferred_element_type=jnp.float32
    ).astype(jnp.bfloat16)
    skel_two = jnp.einsum(
        "mrj,mjk->mrk", join_pairs(skel_one), transfer_two, preferred_element_type=jnp.float32
    ).astype(jnp.bfloat16)
    skeleton = jnp.concatenate([skel_zero, skel_one, skel_two], axis=0)
    far_remote = far_lists.reshape(peer_count, far_count)
    far_owners = far_remote // node_count
    far_ranks = slot_ranks(far_owners)
    far_outgoing, far_wanted = arrivals(far_owners, far_ranks, far_remote, device_index, far_slots)
    far_buffer = (
        jnp.zeros((peer_count * far_slots, R, RANK), jnp.bfloat16)
        .at[far_outgoing]
        .set(skeleton[far_wanted % node_count])
    )
    far_arrived = lax.all_to_all(
        far_buffer.reshape(peer_count, far_slots, R, RANK),
        "leaf",
        split_axis=0,
        concat_axis=0,
        tiled=True,
    )
    my_far = lax.dynamic_index_in_dim(
        far_owners, device_index, 0, keepdims=False
    ) * far_slots + lax.dynamic_index_in_dim(far_ranks, device_index, 0, keepdims=False)
    partners = far_arrived.reshape(peer_count * far_slots, R, RANK)[my_far].reshape(
        node_count, FAR, R, RANK
    )
    leaf_buffer = (
        jnp.zeros((peer_count * near_slots, FEAT + R, LEAF), jnp.bfloat16)
        .at[outgoing]
        .set(blocks[wanted % local_leaves])
    )
    leaf_arrived = lax.all_to_all(
        leaf_buffer.reshape(peer_count, near_slots, FEAT + R, LEAF),
        "leaf",
        split_axis=0,
        concat_axis=0,
        tiled=True,
    )
    sources = leaf_arrived.reshape(peer_count * near_slots, FEAT + R, LEAF)[my_slots]
    per_item = grouped_products(sources, points[item_leaf])
    self_terms = tile_products(blocks, points)
    near = self_terms + jnp.sum(per_item.reshape(local_leaves, NB - 1, R, LEAF), axis=1)
    far = jnp.einsum("nfrk,nfkj->nrj", partners, far_blocks, preferred_element_type=jnp.float32)
    far_zero = far[:local_leaves]
    far_one = far[local_leaves : local_leaves * 3 // 2]
    far_two = far[local_leaves * 3 // 2 :]
    middle = descend(far_two, transfer_two, far_one)
    lowest = descend(middle, transfer_one, far_zero)
    result = near + jnp.einsum(
        "lrk,lak->lra", lowest.astype(jnp.bfloat16), basis, preferred_element_type=jnp.float32
    )
    return result.transpose(1, 0, 2).reshape(R, local_leaves * LEAF)


POINT, EARLY, SKEL, LATE = 0, 1, 2, 3


def visit_orders(rows):
    return [sorted(range(rows), key=lambda row: (abs(row - at), row)) for at in range(rows)]


def tile(source, target, target_half, charge):
    source_f = source.astype(jnp.float32)
    source_half = 0.5 * jnp.sum(source_f * source_f, axis=0, keepdims=True)
    inner = lax.dot_general(
        source, target, (((0,), (0,)), ((), ())), preferred_element_type=jnp.float32
    )
    kernel = jnp.exp(inner - source_half.T - target_half).astype(jnp.bfloat16)
    return jnp.dot(charge, kernel, preferred_element_type=jnp.float32)


def half_square(points):
    points_f = points.astype(jnp.float32)
    return 0.5 * jnp.sum(points_f * points_f, axis=0, keepdims=True)


def whole_kernel(
    rows, parts, source_tab, target_tab, place_tab, pick_tab, give_tab, far_tab, block_tab, coords, rhs, basis_hbm,
    one_hbm, two_hbm, blocks_hbm, out, *scratch
):
    slots = 2 * rows
    points_at = (None,) + scratch[: slots - 1]
    charges_at = (None,) + scratch[slots - 1 : 2 * slots - 2]
    skel_at = scratch[2 * slots - 2 : 2 * slots - 2 + rows]
    (
        given, partners_at, far_out, terms, far_at, basis, one, two, blocks, local_sem, send_sem,
        recv_sem, peer_send_sem, peer_recv_sem,
    ) = scratch[2 * slots - 2 + rows :]
    orders = visit_orders(rows)
    local_leaves, node_count = basis.shape[0], blocks.shape[0] // FAR
    share = coords.shape[1] // parts
    leaf = lax.axis_index("leaf")
    row, side = leaf // 2, leaf % 2
    part = lax.axis_index("rhs")
    across = (row * 2 + 1 - side, part)

    loads = [
        pltpu.make_async_copy(source, target, local_sem.at[which])
        for which, (source, target) in enumerate(
            ((basis_hbm, basis), (one_hbm, one), (two_hbm, two), (blocks_hbm, blocks))
        )
    ]
    for load in loads:
        load.start()

    barrier = pltpu.get_barrier_semaphore()
    mesh_ids = pl.DeviceIdType.MESH
    partners = [across] + [(leaf, (part + away) % parts) for away in range(1, parts)]
    for partner in partners:
        pl.semaphore_signal(barrier, inc=1, device_id=partner, device_id_type=mesh_ids)

    @pl.when(row > 0)
    def _():
        pl.semaphore_signal(barrier, inc=1, device_id=(leaf - 2, part), device_id_type=mesh_ids)

    @pl.when(row < rows - 1)
    def _():
        pl.semaphore_signal(barrier, inc=1, device_id=(leaf + 2, part), device_id_type=mesh_ids)

    ahead = (row + rows - 1) // rows + (2 * rows - 2 - row) // rows
    pl.semaphore_wait(barrier, len(partners) + ahead)

    def mine(points):
        return points.at[:, pl.ds(pl.multiple_of(part * share, share), share), :]

    def far_part(rank):
        return pl.ds(rank * local_leaves, local_leaves)

    def held(kind, slot, own, over):
        if kind == POINT:
            return mine(coords if own and slot == 0 else points_at[slot])
        if kind == SKEL:
            if over:
                return given.at[far_part(slot)] if own else partners_at.at[far_part(slot - 1)]
            return skel_at[slot]
        half = local_leaves // 2
        part_at = pl.ds(0, half) if kind == EARLY else pl.ds(half, local_leaves - half)
        return (rhs if own and slot == 0 else charges_at[slot]).at[part_at]

    def remote(kind, slot, way, to_slot, device):
        return pltpu.make_async_remote_copy(
            src_ref=held(kind, slot, True, way == 2),
            dst_ref=held(kind, to_slot, False, way == 2),
            send_sem=send_sem.at[kind, slot, way],
            recv_sem=recv_sem.at[kind, to_slot],
            device_id=device,
            device_id_type=mesh_ids,
        )

    def to_peer(slot, away):
        return pltpu.make_async_remote_copy(
            src_ref=mine(points_at[slot]),
            dst_ref=mine(points_at[slot]),
            send_sem=peer_send_sem.at[slot, away - 1],
            recv_sem=peer_recv_sem.at[slot, away - 1],
            device_id=(leaf, (part + away) % parts),
            device_id_type=mesh_ids,
        )

    def along(at, kind, slot):
        origin = orders[at][slot]
        found = []
        if origin <= at < rows - 1:
            to_slot = orders[at + 1].index(origin)
            found.append(remote(kind, slot, 0, to_slot, (leaf + 2, part)))
        if origin >= at > 0:
            to_slot = orders[at - 1].index(origin)
            found.append(remote(kind, slot, 1, to_slot, (leaf - 2, part)))
        return found

    def beside(kind, slot):
        return remote(kind, slot, 2, rows + slot, across)

    def arrived(kind, slot):
        if slot < rows:
            remote(kind, 0, 0, slot, across).wait_recv()
        else:
            remote(kind, slot - rows, 2, slot, across).wait_recv()

    def share_points(slot):
        for away in range(1, parts):
            to_peer(slot, away).start()

    def choose(rank):
        def entry(index, carry):
            place = rank * local_leaves + index
            given[place] = skel_at[rank][give_tab[rows * local_leaves - local_leaves + place]]
            if rank > 0:
                taken = place - local_leaves
                partners_at[taken] = skel_at[rank][pick_tab[taken]]
            return carry

        lax.fori_loop(0, local_leaves, entry, 0)

    def start_along(kind, ranks, at):
        for rank in ranks:
            if at != orders[at][rank]:
                arrived(kind, rank)
            for copy in along(at, kind, rank):
                copy.start()

    def open_sends(at):
        for kind in (POINT, EARLY):
            start_along(kind, [0], at)
            beside(kind, 0).start()

    def more_sends(at):
        for kind in (SKEL, LATE):
            start_along(kind, [0], at)
            beside(kind, 0).start()

    def ranks_at(at, distance):
        return [rank for rank in range(rows) if abs(orders[at][rank] - at) == distance]

    def first_phase(at, distance):
        ranks = ranks_at(at, distance)
        for kind in (POINT, EARLY):
            start_along(kind, ranks, at)
            for rank in ranks:
                beside(kind, rank).start()
                if kind == POINT:
                    share_points(rank)

    def second_phase(at, distance):
        ranks = ranks_at(at, distance)
        start_along(SKEL, ranks, at)
        for rank in ranks:
            choose(rank)
        start_along(LATE, ranks, at)
        for rank in ranks:
            beside(SKEL, rank).start()
            beside(LATE, rank).start()

    def by_row(action):
        for at in range(rows):
            pl.when(row == at)(functools.partial(action, at))

    def tiles(slot):
        for away in range(1, parts):
            to_peer(slot, away).wait_recv()
        if slot >= rows:
            arrived(EARLY, slot)
            arrived(LATE, slot)
        first = (slot - 1) * local_leaves

        def entry(index, carry):
            where = first + index
            source = points_at[slot][source_tab[where]]
            target = coords[target_tab[where]]
            charge = charges_at[slot][source_tab[where]]
            terms[where] = tile(source, target, half_square(target), charge)
            return carry

        lax.fori_loop(0, local_leaves, entry, 0, unroll=UNROLL)

    def far_terms(slot):
        first = (slot - 1) * local_leaves

        def entry(index, carry):
            where = first + index
            far_out[where] = jnp.dot(
                partners_at[where], blocks[block_tab[where]], preferred_element_type=jnp.float32
            )
            return carry

        lax.fori_loop(0, local_leaves, entry, 0, unroll=UNROLL)

    by_row(open_sends)

    own_first = (slots - 1) * local_leaves

    def own_entry(index, carry):
        target = coords[index]
        terms[own_first + index] = tile(target, target, half_square(target), rhs[index])
        return carry

    for load in loads[:3]:
        load.wait()
    first_one, first_two = local_leaves, local_leaves * 3 // 2

    def joined(first, transfer):
        left = jnp.dot(
            skel_at[0][first], transfer[:RANK], preferred_element_type=jnp.float32
        )
        right = jnp.dot(
            skel_at[0][first + 1], transfer[RANK:], preferred_element_type=jnp.float32
        )
        return (left + right).astype(jnp.bfloat16)

    for index in range(local_leaves):
        skel_at[0][index] = jnp.dot(
            rhs[index], basis[index], preferred_element_type=jnp.float32
        ).astype(jnp.bfloat16)
    for index in range(first_two - first_one):
        skel_at[0][first_one + index] = joined(2 * index, one[index])
    for index in range(node_count - first_two):
        skel_at[0][first_two + index] = joined(first_one + 2 * index, two[index])
    choose(0)
    lax.fori_loop(0, local_leaves // 2, own_entry, 0, unroll=UNROLL)
    by_row(more_sends)
    lax.fori_loop(local_leaves // 2, local_leaves, own_entry, 0, unroll=UNROLL)
    for distance in range(1, rows):
        by_row(functools.partial(first_phase, distance=distance))
        arrived(POINT, rows + distance - 1)
        share_points(rows + distance - 1)
        if distance > 1:
            tiles(rows + distance - 1)
        by_row(functools.partial(second_phase, distance=distance))
        if distance == 1:
            loads[3].wait()
        tiles(distance)
        far_terms(distance)
        if distance == 1:
            tiles(rows)
        arrived(SKEL, rows + distance - 1)
        far_terms(rows + distance - 1)
    arrived(POINT, slots - 1)
    share_points(slots - 1)
    arrived(SKEL, slots - 1)
    far_terms(slots - 1)

    for node in range(node_count):
        total = far_out[far_tab[node * FAR]]
        for partner in range(1, FAR):
            total = total + far_out[far_tab[node * FAR + partner]]
        far_at[node] = total

    def spread_to(parent, transfer):
        return lax.dot_general(
            parent.astype(jnp.bfloat16), transfer, (((1,), (1,)), ((), ())),
            preferred_element_type=jnp.float32,
        )

    for parent in range(node_count - first_two):
        spread = spread_to(far_at[first_two + parent], two[parent])
        for child in range(2):
            far_at[first_one + 2 * parent + child] += spread[:, child * RANK : (child + 1) * RANK]
    for parent in range(first_two - first_one):
        spread = spread_to(far_at[first_one + parent], one[parent])
        for child in range(2):
            far_at[2 * parent + child] += spread[:, child * RANK : (child + 1) * RANK]

    tiles(slots - 1)

    for index in range(local_leaves):
        total = terms[own_first + index]
        for listed in range(NB - 1):
            total = total + terms[place_tab[index * (NB - 1) + listed]]
        out[:, index * LEAF : (index + 1) * LEAF] = total + spread_to(far_at[index], basis[index])

    def finish(at):
        for kind in (POINT, EARLY, SKEL, LATE):
            for rank in range(rows):
                for copy in along(at, kind, rank):
                    copy.wait_send()

    by_row(finish)
    for rank in range(rows):
        for kind in (POINT, EARLY, SKEL, LATE):
            beside(kind, rank).wait_send()
    for slot in range(1, slots):
        for away in range(1, parts):
            to_peer(slot, away).wait_send()


UNROLL = 4


def on_device(coords, rhs, basis, transfer_one, transfer_two, far_blocks, neighbours, far_lists):
    peer_count = lax.axis_size("leaf")
    whole_lists = peer_count == NB and peer_count % 2 == 0
    even_lists = far_blocks.shape[0] * FAR == (NB - 1) * basis.shape[0]
    even_shares = FEAT % lax.axis_size("rhs") == 0
    route = gathered if whole_lists and even_lists and even_shares else exchanged
    return route(coords, rhs, basis, transfer_one, transfer_two, far_blocks, neighbours, far_lists)


def gathered(coords, rhs, basis, transfer_one, transfer_two, far_blocks, neighbours, far_lists):
    peer_count = lax.axis_size("leaf")
    parts = lax.axis_size("rhs")
    rows = peer_count // 2
    device_index = lax.axis_index("leaf")
    local_leaves = basis.shape[0]
    node_count = far_blocks.shape[0]
    width = rhs.shape[1]
    remote_count = (NB - 1) * local_leaves
    points = coords.reshape(FEAT, local_leaves, LEAF).transpose(1, 0, 2)
    charges = rhs.reshape(R, local_leaves, LEAF).transpose(1, 0, 2)
    orders = visit_orders(rows)
    row, side = device_index // 2, device_index % 2

    def slot_of(owner, side):
        origin, beside = owner // 2, (owner % 2 + side) % 2
        rank = jnp.zeros_like(owner)
        for at in range(rows):
            for place in range(rows):
                matches = jnp.logical_and(row == at, origin == orders[at][place])
                rank = jnp.where(matches, place, rank)
        return beside * rows + rank

    beside_index = device_index + 1 - 2 * side
    lists = jnp.stack(
        [
            neighbours.reshape(peer_count, local_leaves, NB)[:, :, 1:].reshape(peer_count, -1)[
                device_index
            ],
            far_lists.reshape(peer_count, node_count * FAR)[device_index],
            far_lists.reshape(peer_count, node_count * FAR)[beside_index],
        ]
    )
    widths = jnp.array([[local_leaves], [node_count], [node_count]], jnp.int32)
    sides = jnp.stack([side, side, 1 - side])[:, None]
    slot = slot_of(lists // widths, sides)
    position = jnp.arange(remote_count, dtype=jnp.int32)
    earlier = jnp.logical_and(
        slot[:, :, None] == slot[:, None, :], position[None, :] < position[:, None]
    )
    place = (slot - 1) * local_leaves + jnp.sum(earlier, axis=2, dtype=jnp.int32)
    chosen = place[:, None, :] == position[:, None]
    picks = jnp.sum(jnp.where(chosen, (lists % widths)[:, None, :], 0), axis=2)
    entries = jnp.sum(jnp.where(chosen[:2], position, 0), axis=2)
    tables = (
        picks[0], entries[0] // (NB - 1), place[0], picks[1], picks[2], place[1], entries[1]
    )

    smem = pl.BlockSpec(memory_space=pltpu.SMEM)
    vmem = pl.BlockSpec(memory_space=pltpu.VMEM)
    anywhere = pl.BlockSpec(memory_space=pl.ANY)
    remote_slots = peer_count - 1
    bf16 = jnp.bfloat16
    return pl.pallas_call(
        functools.partial(whole_kernel, rows, parts),
        out_shape=jax.ShapeDtypeStruct((R, width), jnp.float32),
        in_specs=[smem] * 7 + [vmem] * 2 + [anywhere] * 4,
        out_specs=vmem,
        scratch_shapes=[pltpu.VMEM((local_leaves, FEAT, LEAF), bf16)] * remote_slots
        + [pltpu.VMEM((local_leaves, R, LEAF), bf16)] * remote_slots
        + [pltpu.VMEM((node_count, R, RANK), bf16)] * rows
        + [
            pltpu.VMEM((rows * local_leaves, R, RANK), bf16),
            pltpu.VMEM((remote_count, R, RANK), bf16),
            pltpu.VMEM((remote_count, R, RANK), jnp.float32),
            pltpu.VMEM((peer_count * local_leaves, R, LEAF), jnp.float32),
            pltpu.VMEM((node_count, R, RANK), jnp.float32),
            pltpu.VMEM(basis.shape, bf16),
            pltpu.VMEM(transfer_one.shape, bf16),
            pltpu.VMEM(transfer_two.shape, bf16),
            pltpu.VMEM((node_count * FAR, RANK, RANK), bf16),
            pltpu.SemaphoreType.DMA((4,)),
            pltpu.SemaphoreType.DMA((4, peer_count, 3)),
            pltpu.SemaphoreType.DMA((4, peer_count)),
            pltpu.SemaphoreType.DMA((peer_count, parts - 1)),
            pltpu.SemaphoreType.DMA((peer_count, parts - 1)),
        ],
        compiler_params=pltpu.CompilerParams(
            collective_id=0, has_side_effects=True, vmem_limit_bytes=56 * 1024 * 1024
        ),
        name="whole",
    )(
        *tables, points, charges, basis, transfer_one, transfer_two,
        far_blocks.reshape(node_count * FAR, RANK, RANK),
    )


def solution(mesh):
    return jax.shard_map(
        on_device,
        mesh=mesh,
        in_specs=(
            P(None, "leaf"),
            P("rhs", "leaf"),
            P("leaf", None, None),
            P("leaf", None, None),
            P("leaf", None, None),
            P("leaf", None, None, None),
            P(),
            P(),
        ),
        out_specs=P("rhs", "leaf"),
        check_vma=False,
    )
```

```python
import functools

import jax
import jax.numpy as jnp
from jax import lax
from jax.experimental import pallas as pl
from jax.experimental.pallas import tpu as pltpu
from jax.sharding import PartitionSpec as P

FEAT = 64
RANK = 256
R = 64
LEAF = 512
NB = 8
FAR = 4


def kernel_tiles(sources, targets):
    inner = jnp.einsum("...fa,...fb->...ab", sources, targets, preferred_element_type=jnp.float32)
    src_f = sources.astype(jnp.float32)
    dst_f = targets.astype(jnp.float32)
    src_sq = jnp.sum(src_f * src_f, axis=-2)
    dst_sq = jnp.sum(dst_f * dst_f, axis=-2)
    return jnp.exp(inner - 0.5 * src_sq[..., :, None] - 0.5 * dst_sq[..., None, :]).astype(
        jnp.bfloat16
    )


def tile_products(sources, targets):
    kernel = kernel_tiles(sources[:, :FEAT], targets)
    return jnp.einsum("gra,gab->grb", sources[:, FEAT:], kernel, preferred_element_type=jnp.float32)


def grouped_products(sources, targets):
    groups = sources.shape[0] // 4
    paired = (
        sources.reshape(groups, 4, sources.shape[1], sources.shape[2]),
        targets.reshape(groups, 4, targets.shape[1], targets.shape[2]),
    )
    outcome = lax.map(lambda couple: tile_products(couple[0], couple[1]), paired)
    return outcome.reshape(sources.shape[0], R, sources.shape[2])


def slot_ranks(owners):
    entry_count = owners.shape[1]
    position = jnp.arange(entry_count, dtype=jnp.int32)
    earlier = position[None, :] < position[:, None]
    matches = owners[:, :, None] == owners[:, None, :]
    return jnp.sum(jnp.logical_and(matches, earlier[None]), axis=2)


def arrivals(owners, ranks, entries, device_index, slot_count):
    entry_count = owners.shape[1]
    located = jnp.nonzero((owners == device_index).reshape(-1), size=entry_count, fill_value=0)[
        0
    ].astype(jnp.int32)
    requester = located // entry_count
    target_slot = requester * slot_count + ranks.reshape(-1)[located]
    return (target_slot, entries.reshape(-1)[located])


def join_pairs(skeleton):
    return skeleton.reshape(-1, 2, R, RANK).transpose(0, 2, 1, 3).reshape(-1, R, 2 * RANK)


def descend(parent, transfer, child_far):
    rounded = parent.astype(jnp.bfloat16)
    spread = jnp.einsum("mrk,mjk->mrj", rounded, transfer, preferred_element_type=jnp.float32)
    spread = spread.reshape(-1, R, 2, RANK).transpose(0, 2, 1, 3).reshape(-1, R, RANK)
    return child_far + spread


def exchanged(coords, rhs, basis, transfer_one, transfer_two, far_blocks, neighbours, far_lists):
    peer_count = lax.axis_size("leaf")
    device_index = lax.axis_index("leaf")
    local_leaves = basis.shape[0]
    node_count = far_blocks.shape[0]
    remote_count = (NB - 1) * local_leaves
    near_slots = (remote_count + peer_count - 2) // (peer_count - 1)
    far_count = node_count * FAR
    far_slots = (far_count + peer_count - 2) // (peer_count - 1)
    points = coords.reshape(FEAT, local_leaves, LEAF).transpose(1, 0, 2)
    charges = rhs.reshape(R, local_leaves, LEAF).transpose(1, 0, 2)
    blocks = jnp.concatenate([points, charges], axis=1)
    remote = neighbours.reshape(peer_count, local_leaves, NB)[:, :, 1:].reshape(
        peer_count, remote_count
    )
    owners = remote // local_leaves
    ranks = slot_ranks(owners)
    my_owners = lax.dynamic_index_in_dim(owners, device_index, 0, keepdims=False)
    my_ranks = lax.dynamic_index_in_dim(ranks, device_index, 0, keepdims=False)
    my_slots = my_owners * near_slots + my_ranks
    outgoing, wanted = arrivals(owners, ranks, remote, device_index, near_slots)
    item_leaf = jnp.arange(remote_count, dtype=jnp.int32) // (NB - 1)
    skel_zero = jnp.einsum(
        "lra,lak->lrk", charges, basis, preferred_element_type=jnp.float32
    ).astype(jnp.bfloat16)
    skel_one = jnp.einsum(
        "mrj,mjk->mrk", join_pairs(skel_zero), transfer_one, preferred_element_type=jnp.float32
    ).astype(jnp.bfloat16)
    skel_two = jnp.einsum(
        "mrj,mjk->mrk", join_pairs(skel_one), transfer_two, preferred_element_type=jnp.float32
    ).astype(jnp.bfloat16)
    skeleton = jnp.concatenate([skel_zero, skel_one, skel_two], axis=0)
    far_remote = far_lists.reshape(peer_count, far_count)
    far_owners = far_remote // node_count
    far_ranks = slot_ranks(far_owners)
    far_outgoing, far_wanted = arrivals(far_owners, far_ranks, far_remote, device_index, far_slots)
    far_buffer = (
        jnp.zeros((peer_count * far_slots, R, RANK), jnp.bfloat16)
        .at[far_outgoing]
        .set(skeleton[far_wanted % node_count])
    )
    far_arrived = lax.all_to_all(
        far_buffer.reshape(peer_count, far_slots, R, RANK),
        "leaf",
        split_axis=0,
        concat_axis=0,
        tiled=True,
    )
    my_far = lax.dynamic_index_in_dim(
        far_owners, device_index, 0, keepdims=False
    ) * far_slots + lax.dynamic_index_in_dim(far_ranks, device_index, 0, keepdims=False)
    partners = far_arrived.reshape(peer_count * far_slots, R, RANK)[my_far].reshape(
        node_count, FAR, R, RANK
    )
    leaf_buffer = (
        jnp.zeros((peer_count * near_slots, FEAT + R, LEAF), jnp.bfloat16)
        .at[outgoing]
        .set(blocks[wanted % local_leaves])
    )
    leaf_arrived = lax.all_to_all(
        leaf_buffer.reshape(peer_count, near_slots, FEAT + R, LEAF),
        "leaf",
        split_axis=0,
        concat_axis=0,
        tiled=True,
    )
    sources = leaf_arrived.reshape(peer_count * near_slots, FEAT + R, LEAF)[my_slots]
    per_item = grouped_products(sources, points[item_leaf])
    self_terms = tile_products(blocks, points)
    near = self_terms + jnp.sum(per_item.reshape(local_leaves, NB - 1, R, LEAF), axis=1)
    far = jnp.einsum("nfrk,nfkj->nrj", partners, far_blocks, preferred_element_type=jnp.float32)
    far_zero = far[:local_leaves]
    far_one = far[local_leaves : local_leaves * 3 // 2]
    far_two = far[local_leaves * 3 // 2 :]
    middle = descend(far_two, transfer_two, far_one)
    lowest = descend(middle, transfer_one, far_zero)
    result = near + jnp.einsum(
        "lrk,lak->lra", lowest.astype(jnp.bfloat16), basis, preferred_element_type=jnp.float32
    )
    return result.transpose(1, 0, 2).reshape(R, local_leaves * LEAF)


POINT, EARLY, SKEL, LATE = 0, 1, 2, 3


def visit_orders(rows):
    return [sorted(range(rows), key=lambda row: (abs(row - at), row)) for at in range(rows)]


def tile(source, target, target_half, charge):
    source_f = source.astype(jnp.float32)
    source_half = 0.5 * jnp.sum(source_f * source_f, axis=0, keepdims=True)
    inner = lax.dot_general(
        source, target, (((0,), (0,)), ((), ())), preferred_element_type=jnp.float32
    )
    kernel = jnp.exp(inner - source_half.T - target_half).astype(jnp.bfloat16)
    return jnp.dot(charge, kernel, preferred_element_type=jnp.float32)


def half_square(points):
    points_f = points.astype(jnp.float32)
    return 0.5 * jnp.sum(points_f * points_f, axis=0, keepdims=True)


def whole_kernel(
    rows, parts, picks, places, entries, coords_hbm, rhs_hbm, basis_hbm,
    one_hbm, two_hbm, blocks_hbm, out, *scratch
):
    slots = 2 * rows
    points_at = (None,) + scratch[: slots - 1]
    charges_at = (None,) + scratch[slots - 1 : 2 * slots - 2]
    skel_at = scratch[2 * slots - 2 : 2 * slots - 2 + rows]
    (
        coords, rhs, given, partners_at, far_out, terms, far_at, basis, one, two, blocks, local_sem, leaf_sem, send_sem,
        recv_sem, peer_send_sem, peer_recv_sem,
    ) = scratch[2 * slots - 2 + rows :]
    orders = visit_orders(rows)
    local_leaves, node_count = basis.shape[0], blocks.shape[0] // FAR
    share = coords.shape[1] // parts
    leaf = lax.axis_index("leaf")
    row, side = leaf // 2, leaf % 2
    part = lax.axis_index("rhs")
    across = (row * 2 + 1 - side, part)

    loads = [
        pltpu.make_async_copy(source, target, local_sem.at[which])
        for which, (source, target) in enumerate(
            ((basis_hbm, basis), (one_hbm, one), (two_hbm, two), (blocks_hbm, blocks))
        )
    ]
    leaf_loads = [
        pltpu.make_async_copy(
            source.at[:, pl.ds(index * LEAF, LEAF)], target.at[index], leaf_sem.at[which, index]
        )
        for which, (source, target) in enumerate(((coords_hbm, coords), (rhs_hbm, rhs)))
        for index in range(local_leaves)
    ]
    for load in leaf_loads + loads:
        load.start()

    barrier = pltpu.get_barrier_semaphore()
    mesh_ids = pl.DeviceIdType.MESH
    partners = [across] + [(leaf, (part + away) % parts) for away in range(1, parts)]
    for partner in partners:
        pl.semaphore_signal(barrier, inc=1, device_id=partner, device_id_type=mesh_ids)

    @pl.when(row > 0)
    def _():
        pl.semaphore_signal(barrier, inc=1, device_id=(leaf - 2, part), device_id_type=mesh_ids)

    @pl.when(row < rows - 1)
    def _():
        pl.semaphore_signal(barrier, inc=1, device_id=(leaf + 2, part), device_id_type=mesh_ids)

    ahead = (row + rows - 1) // rows + (2 * rows - 2 - row) // rows
    pl.semaphore_wait(barrier, len(partners) + ahead)

    def mine(points):
        return points.at[:, pl.ds(pl.multiple_of(part * share, share), share), :]

    def far_part(rank):
        return pl.ds(rank * local_leaves, local_leaves)

    def held(kind, slot, own, over):
        if kind == POINT:
            return mine(coords if own and slot == 0 else points_at[slot])
        if kind == SKEL:
            if over:
                return given.at[far_part(slot)] if own else partners_at.at[far_part(slot - 1)]
            return skel_at[slot]
        half = local_leaves // 2
        part_at = pl.ds(0, half) if kind == EARLY else pl.ds(half, local_leaves - half)
        return (rhs if own and slot == 0 else charges_at[slot]).at[part_at]

    def remote(kind, slot, way, to_slot, device):
        return pltpu.make_async_remote_copy(
            src_ref=held(kind, slot, True, way == 2),
            dst_ref=held(kind, to_slot, False, way == 2),
            send_sem=send_sem.at[kind, slot, way],
            recv_sem=recv_sem.at[kind, to_slot],
            device_id=device,
            device_id_type=mesh_ids,
        )

    def to_peer(slot, away):
        return pltpu.make_async_remote_copy(
            src_ref=mine(points_at[slot]),
            dst_ref=mine(points_at[slot]),
            send_sem=peer_send_sem.at[slot, away - 1],
            recv_sem=peer_recv_sem.at[slot, away - 1],
            device_id=(leaf, (part + away) % parts),
            device_id_type=mesh_ids,
        )

    def along(at, kind, slot):
        origin = orders[at][slot]
        found = []
        if origin <= at < rows - 1:
            to_slot = orders[at + 1].index(origin)
            found.append(remote(kind, slot, 0, to_slot, (leaf + 2, part)))
        if origin >= at > 0:
            to_slot = orders[at - 1].index(origin)
            found.append(remote(kind, slot, 1, to_slot, (leaf - 2, part)))
        return found

    def beside(kind, slot):
        return remote(kind, slot, 2, rows + slot, across)

    def arrived(kind, slot):
        if slot < rows:
            remote(kind, 0, 0, slot, across).wait_recv()
        else:
            remote(kind, slot - rows, 2, slot, across).wait_recv()

    def share_points(slot):
        for away in range(1, parts):
            to_peer(slot, away).start()

    def choose(rank):
        def entry(index, carry):
            place = rank * local_leaves + index
            given[place] = skel_at[rank][picks[2, rows * local_leaves - local_leaves + place]]
            if rank > 0:
                taken = place - local_leaves
                partners_at[taken] = skel_at[rank][picks[1, taken]]
            return carry

        lax.fori_loop(0, local_leaves, entry, 0)

    def start_along(kind, ranks, at):
        for rank in ranks:
            if at != orders[at][rank]:
                arrived(kind, rank)
            for copy in along(at, kind, rank):
                copy.start()

    def open_sends(at):
        for kind in (POINT, EARLY):
            start_along(kind, [0], at)
            beside(kind, 0).start()

    def more_sends(at):
        for kind in (SKEL, LATE):
            start_along(kind, [0], at)
            beside(kind, 0).start()

    def ranks_at(at, distance):
        return [rank for rank in range(rows) if abs(orders[at][rank] - at) == distance]

    def first_phase(at, distance):
        ranks = ranks_at(at, distance)
        for kind in (POINT, EARLY):
            start_along(kind, ranks, at)
            for rank in ranks:
                beside(kind, rank).start()
                if kind == POINT:
                    share_points(rank)

    def second_phase(at, distance):
        ranks = ranks_at(at, distance)
        start_along(SKEL, ranks, at)
        for rank in ranks:
            choose(rank)
        start_along(LATE, ranks, at)
        for rank in ranks:
            beside(SKEL, rank).start()
            beside(LATE, rank).start()

    def by_row(action):
        for at in range(rows):
            pl.when(row == at)(functools.partial(action, at))

    def tiles(slot):
        for away in range(1, parts):
            to_peer(slot, away).wait_recv()
        if slot >= rows:
            arrived(EARLY, slot)
            arrived(LATE, slot)
        first = (slot - 1) * local_leaves

        def entry(index, carry):
            where = first + index
            source = points_at[slot][picks[0, where]]
            target = coords[entries[0, where]]
            charge = charges_at[slot][picks[0, where]]
            terms[where] = tile(source, target, half_square(target), charge)
            return carry

        lax.fori_loop(0, local_leaves, entry, 0, unroll=UNROLL)

    def far_terms(slot):
        first = (slot - 1) * local_leaves

        def entry(index, carry):
            where = first + index
            far_out[where] = jnp.dot(
                partners_at[where], blocks[entries[1, where]], preferred_element_type=jnp.float32
            )
            return carry

        lax.fori_loop(0, local_leaves, entry, 0, unroll=UNROLL)

    for load in leaf_loads:
        load.wait()
    by_row(open_sends)

    own_first = (slots - 1) * local_leaves

    def own_entry(index, carry):
        target = coords[index]
        terms[own_first + index] = tile(target, target, half_square(target), rhs[index])
        return carry

    for load in loads[:3]:
        load.wait()
    first_one, first_two = local_leaves, local_leaves * 3 // 2

    def joined(first, transfer):
        left = jnp.dot(
            skel_at[0][first], transfer[:RANK], preferred_element_type=jnp.float32
        )
        right = jnp.dot(
            skel_at[0][first + 1], transfer[RANK:], preferred_element_type=jnp.float32
        )
        return (left + right).astype(jnp.bfloat16)

    for index in range(local_leaves):
        skel_at[0][index] = jnp.dot(
            rhs[index], basis[index], preferred_element_type=jnp.float32
        ).astype(jnp.bfloat16)
    for index in range(first_two - first_one):
        skel_at[0][first_one + index] = joined(2 * index, one[index])
    for index in range(node_count - first_two):
        skel_at[0][first_two + index] = joined(first_one + 2 * index, two[index])
    choose(0)
    lax.fori_loop(0, local_leaves // 2, own_entry, 0, unroll=UNROLL)
    by_row(more_sends)
    lax.fori_loop(local_leaves // 2, local_leaves, own_entry, 0, unroll=UNROLL)
    for distance in range(1, rows):
        by_row(functools.partial(first_phase, distance=distance))
        arrived(POINT, rows + distance - 1)
        share_points(rows + distance - 1)
        if distance > 1:
            tiles(rows + distance - 1)
        by_row(functools.partial(second_phase, distance=distance))
        if distance == 1:
            loads[3].wait()
        tiles(distance)
        far_terms(distance)
        if distance == 1:
            tiles(rows)
        arrived(SKEL, rows + distance - 1)
        far_terms(rows + distance - 1)
    arrived(POINT, slots - 1)
    share_points(slots - 1)
    arrived(SKEL, slots - 1)
    far_terms(slots - 1)

    for node in range(node_count):
        total = far_out[places[1, node * FAR]]
        for partner in range(1, FAR):
            total = total + far_out[places[1, node * FAR + partner]]
        far_at[node] = total

    def spread_to(parent, transfer):
        return lax.dot_general(
            parent.astype(jnp.bfloat16), transfer, (((1,), (1,)), ((), ())),
            preferred_element_type=jnp.float32,
        )

    for parent in range(node_count - first_two):
        spread = spread_to(far_at[first_two + parent], two[parent])
        for child in range(2):
            far_at[first_one + 2 * parent + child] += spread[:, child * RANK : (child + 1) * RANK]
    for parent in range(first_two - first_one):
        spread = spread_to(far_at[first_one + parent], one[parent])
        for child in range(2):
            far_at[2 * parent + child] += spread[:, child * RANK : (child + 1) * RANK]

    tiles(slots - 1)

    for index in range(local_leaves):
        total = terms[own_first + index]
        for listed in range(NB - 1):
            total = total + terms[places[0, index * (NB - 1) + listed]]
        out[:, index * LEAF : (index + 1) * LEAF] = total + spread_to(far_at[index], basis[index])

    def finish(at):
        for kind in (POINT, EARLY, SKEL, LATE):
            for rank in range(rows):
                for copy in along(at, kind, rank):
                    copy.wait_send()

    by_row(finish)
    for rank in range(rows):
        for kind in (POINT, EARLY, SKEL, LATE):
            beside(kind, rank).wait_send()
    for slot in range(1, slots):
        for away in range(1, parts):
            to_peer(slot, away).wait_send()


UNROLL = 4


def on_device(coords, rhs, basis, transfer_one, transfer_two, far_blocks, neighbours, far_lists):
    peer_count = lax.axis_size("leaf")
    whole_lists = peer_count == NB and peer_count % 2 == 0
    even_lists = far_blocks.shape[0] * FAR == (NB - 1) * basis.shape[0]
    even_shares = FEAT % lax.axis_size("rhs") == 0
    route = gathered if whole_lists and even_lists and even_shares else exchanged
    return route(coords, rhs, basis, transfer_one, transfer_two, far_blocks, neighbours, far_lists)


def gathered(coords, rhs, basis, transfer_one, transfer_two, far_blocks, neighbours, far_lists):
    peer_count = lax.axis_size("leaf")
    parts = lax.axis_size("rhs")
    rows = peer_count // 2
    device_index = lax.axis_index("leaf")
    local_leaves = basis.shape[0]
    node_count = far_blocks.shape[0]
    width = rhs.shape[1]
    remote_count = (NB - 1) * local_leaves
    orders = visit_orders(rows)
    row, side = device_index // 2, device_index % 2

    def slot_of(owner, side):
        origin, beside = owner // 2, (owner % 2 + side) % 2
        rank = jnp.zeros_like(owner)
        for at in range(rows):
            for place in range(rows):
                matches = jnp.logical_and(row == at, origin == orders[at][place])
                rank = jnp.where(matches, place, rank)
        return beside * rows + rank

    beside_index = device_index + 1 - 2 * side
    lists = jnp.stack(
        [
            neighbours.reshape(peer_count, local_leaves, NB)[:, :, 1:].reshape(peer_count, -1)[
                device_index
            ],
            far_lists.reshape(peer_count, node_count * FAR)[device_index],
            far_lists.reshape(peer_count, node_count * FAR)[beside_index],
        ]
    )
    widths = jnp.array([[local_leaves], [node_count], [node_count]], jnp.int32)
    sides = jnp.stack([side, side, 1 - side])[:, None]
    slot = slot_of(lists // widths, sides)
    position = jnp.arange(remote_count, dtype=jnp.int32)
    earlier = jnp.logical_and(
        slot[:, :, None] == slot[:, None, :], position[None, :] < position[:, None]
    )
    place = (slot - 1) * local_leaves + jnp.sum(earlier, axis=2, dtype=jnp.int32)
    chosen = place[:, None, :] == position[:, None]
    picks = jnp.sum(jnp.where(chosen, (lists % widths)[:, None, :], 0), axis=2)
    entries = jnp.sum(jnp.where(chosen[:2], position, 0), axis=2)
    divisors = jnp.array([[NB - 1], [1]], jnp.int32)
    tables = (picks, place, entries // divisors)

    smem = pl.BlockSpec(memory_space=pltpu.SMEM)
    vmem = pl.BlockSpec(memory_space=pltpu.VMEM)
    anywhere = pl.BlockSpec(memory_space=pl.ANY)
    remote_slots = peer_count - 1
    bf16 = jnp.bfloat16
    return pl.pallas_call(
        functools.partial(whole_kernel, rows, parts),
        out_shape=jax.ShapeDtypeStruct((R, width), jnp.float32),
        in_specs=[smem] * 3 + [anywhere] * 6,
        out_specs=vmem,
        scratch_shapes=[pltpu.VMEM((local_leaves, FEAT, LEAF), bf16)] * remote_slots
        + [pltpu.VMEM((local_leaves, R, LEAF), bf16)] * remote_slots
        + [pltpu.VMEM((node_count, R, RANK), bf16)] * rows
        + [
            pltpu.VMEM((local_leaves, FEAT, LEAF), bf16),
            pltpu.VMEM((local_leaves, R, LEAF), bf16),
            pltpu.VMEM((rows * local_leaves, R, RANK), bf16),
            pltpu.VMEM((remote_count, R, RANK), bf16),
            pltpu.VMEM((remote_count, R, RANK), jnp.float32),
            pltpu.VMEM((peer_count * local_leaves, R, LEAF), jnp.float32),
            pltpu.VMEM((node_count, R, RANK), jnp.float32),
            pltpu.VMEM(basis.shape, bf16),
            pltpu.VMEM(transfer_one.shape, bf16),
            pltpu.VMEM(transfer_two.shape, bf16),
            pltpu.VMEM((node_count * FAR, RANK, RANK), bf16),
            pltpu.SemaphoreType.DMA((4,)),
            pltpu.SemaphoreType.DMA((2, local_leaves)),
            pltpu.SemaphoreType.DMA((4, peer_count, 3)),
            pltpu.SemaphoreType.DMA((4, peer_count)),
            pltpu.SemaphoreType.DMA((peer_count, parts - 1)),
            pltpu.SemaphoreType.DMA((peer_count, parts - 1)),
        ],
        compiler_params=pltpu.CompilerParams(
            collective_id=0, has_side_effects=True, vmem_limit_bytes=56 * 1024 * 1024
        ),
        name="whole",
    )(
        *tables, coords, rhs, basis, transfer_one, transfer_two,
        far_blocks.reshape(node_count * FAR, RANK, RANK),
    )


def solution(mesh):
    return jax.shard_map(
        on_device,
        mesh=mesh,
        in_specs=(
            P(None, "leaf"),
            P("rhs", "leaf"),
            P("leaf", None, None),
            P("leaf", None, None),
            P("leaf", None, None),
            P("leaf", None, None, None),
            P(),
            P(),
        ),
        out_specs=P("rhs", "leaf"),
        check_vma=False,
    )
```
